32 devices in a mesh: ctx: 8 (over z, x), head: 4 (over y, core).
Axes of the slice: x: 2, y: 2, z: 4, core: 2. Of those that a mesh axis runs over, the one named last changes fastest.
Arguments:
- queries: bfloat16 [3072, 8192], P(('ctx', 'head')), may hold values from -6 to 6
- keys: bfloat16 [3072, 1024], P(('ctx', 'head')), may hold values from -6 to 6
- values: bfloat16 [3072, 1024], P(('ctx', 'head')), may hold values from -6 to 6
- attn_out: bfloat16 [3072, 8192], P('ctx', 'head'), may hold values from -6 to 6
- out_grad: bfloat16 [3072, 8192], P('ctx', 'head'), may hold values from -12 to 12
- log_sum: float32 [64, 3072], P('head', 'ctx'), as said below
- file_ids: int32 [3072], P('ctx'), may hold values from 0 to 7, as said below
Outputs:
- q_grad: bfloat16 [3072, 8192], P(('ctx', 'head'))
- k_grad: bfloat16 [3072, 1024], P(('ctx', 'head'))
- v_grad: bfloat16 [3072, 1024], P(('ctx', 'head'))
The draws below stay inside these ranges and needn't reach their ends.
Inputs may be any that keep to these rules, and one draw needn't show every extreme that they name: file_ids never fall along the tokens, so each file's tokens are consecutive; each of the 8 files holds 1 to 1536 tokens, and the first file holds exactly 1536. log_sum is positive.
All inputs are finite; a program needn't handle non-finite values.
Results may differ from the reference program's by a relative error of at most 0.0053.
Values may be sent and summed in bfloat16 or wider, within the bound.
No kernel may reach another device: no remote copies, remote signals or barrier semaphores. Data moves between devices by JAX's collectives and lax.ppermute only.
A program may use at most 64 MiB of HBM per device.

```python
import math
import jax
import jax.numpy as jnp
from jax import lax

HEADS = 64
KVH = 8
DH = 128
TOK_DEV = 384
NFILES = 8
TOKENS = 3072
MAXFILE = 1536
N_CTX = 8


def file_layout(key):
    base_key = jax.random.fold_in(key, 7)
    rest_tokens = TOKENS - MAXFILE
    shuffled = jax.random.permutation(jax.random.fold_in(base_key, 1), rest_tokens - 1)
    cut_points = jnp.sort(shuffled[:NFILES - 2].astype(jnp.int32) + 1)
    piece_edges = jnp.concatenate([jnp.zeros((1,), jnp.int32), cut_points, jnp.full((1,), rest_tokens, jnp.int32)])
    piece_lengths = piece_edges[1:] - piece_edges[:-1]
    file_index = jnp.arange(NFILES, dtype=jnp.int32)
    right_choice = piece_lengths[jnp.clip(file_index - 1, 0, NFILES - 2)]
    file_lengths = jnp.where(file_index == 0, MAXFILE, right_choice).astype(jnp.int32)
    file_starts = (jnp.cumsum(file_lengths) - file_lengths).astype(jnp.int32)
    tokens = jnp.arange(TOKENS, dtype=jnp.int32)
    token_files = jnp.sum((tokens[:, None] >= file_starts[None, 1:]).astype(jnp.int32), axis=1).astype(jnp.int32)
    in_file = tokens - file_starts[token_files]
    return (token_files, in_file)


def draw_file_ids(key, part):
    return file_layout(key)[0]


def draw_log_sum(key, part):
    in_file = file_layout(key)[1]
    jitter_key = jax.random.fold_in(key, 11)
    jitter = jnp.clip(0.15 * jax.random.normal(jitter_key, (HEADS, TOKENS), jnp.float32), -0.35, 0.35)
    return jnp.log(in_file.astype(jnp.float32)[None, :] + 1.0) + 0.5 + jitter


def steps_of(own_key, dims, split, smallest, largest):
    factor_of, own = 1.0, jax.random.fold_in(own_key, 6)
    for axis_at, blocks in split:
        steps = jnp.exp(jax.random.uniform(jax.random.fold_in(own, axis_at), (blocks,), jnp.float32, smallest / len(split), largest / len(split)))
        factor_of = factor_of * jnp.repeat(steps, dims[axis_at] // blocks).reshape([-1 if axis == axis_at else 1 for axis in range(len(dims))])
    return factor_of


def normal_values(rng, dims, spread, reach, shards=(), held_as=jnp.bfloat16):
    loudness = steps_of(rng, dims, shards, -0.22, 0.18) if shards else 1.0
    entries = jax.random.normal(rng, dims, jnp.float32) * spread * loudness
    return jnp.minimum(jnp.maximum(entries, -reach), reach).astype(held_as)


def setup_inputs(seed: int = 0) -> dict:
    streams_of = jax.random.split(jax.random.key(seed), 8)
    queries = normal_values(streams_of[0], (TOKENS, HEADS * DH), 1.0, 6.0, ((0, 32),))
    keys = normal_values(streams_of[1], (TOKENS, KVH * DH), 1.0, 6.0, ((0, 32),))
    values = normal_values(streams_of[2], (TOKENS, KVH * DH), 1.0, 6.0, ((0, 32),))
    attn_out = normal_values(streams_of[3], (TOKENS, HEADS * DH), 0.5, 6.0, ((0, 8), (1, 4)))
    out_grad = normal_values(streams_of[4], (TOKENS, HEADS * DH), 2.0, 12.0, ((0, 8), (1, 4)))
    log_sum = draw_log_sum(jax.random.fold_in(streams_of[7], 71), 0)
    file_ids = draw_file_ids(jax.random.fold_in(streams_of[7], 71), 0)
    return dict(queries=queries, keys=keys, values=values, attn_out=attn_out, out_grad=out_grad, log_sum=log_sum, file_ids=file_ids)


def tile_grads(q_four, g_four, lse_three, delta_three, key_part, value_part, allowed):
    score_scale = 1.0 / math.sqrt(DH)
    scores = jnp.einsum('rkgd,ckd->kgrc', q_four, key_part) * score_scale
    attn_probs = jnp.exp(jnp.where(allowed[None, None], scores - lse_three[..., None], -1e+30))
    probs_low = lax.optimization_barrier(attn_probs.astype(jnp.bfloat16)).astype(jnp.float32)
    dprobs = jnp.einsum('rkgd,ckd->kgrc', g_four, value_part)
    dscores_low = lax.optimization_barrier((attn_probs * (dprobs - delta_three[..., None])).astype(jnp.bfloat16)).astype(jnp.float32)
    q_part = jnp.einsum('kgrc,ckd->rkgd', dscores_low, key_part)
    k_part = jnp.einsum('kgrc,rkgd->ckd', dscores_low, q_four)
    v_part = jnp.einsum('kgrc,rkgd->ckd', probs_low, g_four)
    return (q_part, k_part, v_part)

def reference(queries, keys, values, attn_out, out_grad, log_sum, file_ids):
    group_size = HEADS // KVH
    score_scale = 1.0 / math.sqrt(DH)
    block_rows = TOK_DEV
    reach_back = N_CTX // 2
    q_all = queries.reshape(TOKENS, KVH, group_size, DH)
    g_all = out_grad.reshape(TOKENS, KVH, group_size, DH)
    o_all = attn_out.reshape(TOKENS, KVH, group_size, DH)
    key_all = keys.reshape(TOKENS, KVH, DH)
    value_all = values.reshape(TOKENS, KVH, DH)
    lse_all = log_sum.reshape(KVH, group_size, TOKENS)
    positions = jnp.arange(TOKENS, dtype=jnp.int32)

    def query_block(outer_state, block_index):
        k_sum, v_sum = outer_state
        row_start = (block_index * block_rows).astype(jnp.int32)
        q_blk = lax.dynamic_slice_in_dim(q_all, row_start, block_rows, 0).astype(jnp.float32)
        g_blk = lax.dynamic_slice_in_dim(g_all, row_start, block_rows, 0).astype(jnp.float32)
        o_blk = lax.dynamic_slice_in_dim(o_all, row_start, block_rows, 0).astype(jnp.float32)
        lse_blk = lax.dynamic_slice_in_dim(lse_all, row_start, block_rows, 2)
        delta_blk = jnp.transpose(lax.optimization_barrier(jnp.sum(g_blk * o_blk, axis=-1)), (1, 2, 0))
        ids_query = lax.dynamic_slice_in_dim(file_ids, row_start, block_rows, 0)
        pos_query = lax.dynamic_slice_in_dim(positions, row_start, block_rows, 0)

        def key_block(step_index, inner_state):
            q_acc, k_acc, v_acc = inner_state
            key_block_index = (block_index - step_index).astype(jnp.int32)
            key_start = (jnp.maximum(key_block_index, 0) * block_rows).astype(jnp.int32)
            k_blk = lax.dynamic_slice_in_dim(key_all, key_start, block_rows, 0).astype(jnp.float32)
            v_blk = lax.dynamic_slice_in_dim(value_all, key_start, block_rows, 0).astype(jnp.float32)
            ids_key = lax.dynamic_slice_in_dim(file_ids, key_start, block_rows, 0)
            pos_key = lax.dynamic_slice_in_dim(positions, key_start, block_rows, 0)
            allowed = (ids_query[:, None] == ids_key[None, :]) & (pos_key[None, :] <= pos_query[:, None]) & (key_block_index >= 0)

            def compute():
                q_part, k_part, v_part = tile_grads(q_blk, g_blk, lse_blk, delta_blk, k_blk, v_blk, allowed)
                k_new = lax.dynamic_update_slice_in_dim(k_acc, lax.dynamic_slice_in_dim(k_acc, key_start, block_rows, 0) + k_part, key_start, 0)
                v_new = lax.dynamic_update_slice_in_dim(v_acc, lax.dynamic_slice_in_dim(v_acc, key_start, block_rows, 0) + v_part, key_start, 0)
                return (q_acc + q_part, k_new, v_new)

            def skipped():
                return (q_acc, k_acc, v_acc)
            return lax.cond(jnp.any(allowed), compute, skipped)
        start_state = (jnp.zeros((block_rows, KVH, group_size, DH), jnp.float32), k_sum, v_sum)
        q_acc, k_sum, v_sum = lax.fori_loop(0, reach_back + 1, key_block, start_state)
        return ((k_sum, v_sum), (q_acc * score_scale).astype(jnp.bfloat16))
    zero_grads = jnp.zeros((TOKENS, KVH, DH), jnp.float32)
    sums, q_blocks = lax.scan(query_block, (zero_grads, zero_grads), jnp.arange(N_CTX, dtype=jnp.int32))
    q_grad = q_blocks.reshape(TOKENS, HEADS * DH)
    k_grad = (sums[0] * score_scale).astype(jnp.bfloat16).reshape(TOKENS, KVH * DH)
    v_grad = sums[1].astype(jnp.bfloat16).reshape(TOKENS, KVH * DH)
    return (q_grad, k_grad, v_grad)
```

```python
import math

import jax
import jax.numpy as jnp
from jax import lax
from jax.experimental import pallas as pl
from jax.experimental.pallas import tpu as pltpu
from jax.sharding import PartitionSpec as P

DH = 128
SCORE_SCALE = 1.0 / math.sqrt(DH)
LOG2E = math.log2(math.e)
NT = (((1,), (1,)), ((), ()))
NN = (((1,), (0,)), ((), ()))
TN = (((0,), (0,)), ((), ()))


def dot(a, b, dims):
    return lax.dot_general(a, b, dims, preferred_element_type=jnp.float32)


def delta_kernel(grad_ref, out_ref, delta_ref):
    heads = delta_ref.shape[0]
    for head in range(heads):
        cols = slice(head * DH, (head + 1) * DH)
        prod = grad_ref[:, cols].astype(jnp.float32) * out_ref[:, cols].astype(jnp.float32)
        delta_ref[head : head + 1, :] = jnp.sum(jnp.transpose(prod), axis=0, keepdims=True)


def row_deltas(out_grad, attn_out, heads):
    rows = out_grad.shape[0]
    return pl.pallas_call(
        delta_kernel,
        out_shape=jax.ShapeDtypeStruct((heads, rows), jnp.float32),
        compiler_params=pltpu.CompilerParams(vmem_limit_bytes=32 << 20),
        cost_estimate=pl.CostEstimate(
            flops=4 * rows * heads * DH, bytes_accessed=4 * rows * heads * DH, transcendentals=0
        ),
        name="row_deltas",
    )(out_grad, attn_out)


def grads_kernel(half, kv_heads, group, info_ref, *refs):
    start_ref, q_ref, g_ref, lse_ref, delta_ref, kv_own = refs[:6]
    kv_in = refs[6 : 6 + half - 1]
    dq_ref, dkv_own = refs[5 + half : 7 + half]
    dkv_out = refs[7 + half : 6 + 2 * half]
    kv_buf, dkv_buf, dq_acc, dk_acc, dv_acc, bias, in_sem, out_sem = refs[6 + 2 * half :]
    rows = q_ref.shape[0]
    own = info_ref[0]
    first_start = info_ref[1]
    last_start = info_ref[2]
    base = info_ref[3]

    for step in range(1, half):
        @pl.when((own ^ step) < own)
        def _():
            pltpu.make_async_copy(kv_in[step - 1], kv_buf.at[step - 1], in_sem.at[step - 1]).start()

    def tile(load_kv, masked, first, store):
        def per_kv_head(kv_head, _):
            k_cols = pl.ds(pl.multiple_of(kv_head * DH, DH), DH)
            v_cols = pl.ds(pl.multiple_of((kv_heads + kv_head) * DH, DH), DH)
            key = load_kv(k_cols)
            value = load_kv(v_cols)
            for member in range(group):
                head = kv_head * group + member
                cols = pl.ds(pl.multiple_of(head * DH, DH), DH)
                query = q_ref[:, cols]
                grad = g_ref[:, cols]
                scores = dot(key, query, NT) * (SCORE_SCALE * LOG2E) - lse_ref[pl.ds(head, 1), :]
                if masked:
                    scores = scores + bias[...]
                probs = jnp.exp2(scores)
                dprobs = dot(value, grad, NT)
                dscores = (probs * (dprobs - delta_ref[pl.ds(head, 1), :])).astype(jnp.bfloat16)
                dv_part = dot(probs.astype(jnp.bfloat16), grad, NN)
                dk_part = dot(dscores, query, NN)
                dq_part = dot(dscores, key, TN)
                if member == 0:
                    dv_acc[...] = dv_part
                    dk_acc[...] = dk_part
                else:
                    dv_acc[...] += dv_part
                    dk_acc[...] += dk_part
                if first:
                    dq_acc[:, cols] = dq_part
                else:
                    dq_acc[:, cols] += dq_part
            store(k_cols, dk_acc[...] * SCORE_SCALE)
            store(v_cols, dv_acc[...])
            return 0

        lax.fori_loop(0, kv_heads, per_kv_head, 0)

    def set_bias(block):
        key_pos = (base + block) * rows + lax.broadcasted_iota(jnp.int32, (rows, rows), 0)
        query_pos = (base + own) * rows + lax.broadcasted_iota(jnp.int32, (rows, rows), 1)
        allowed = (key_pos >= start_ref[...]) & (key_pos <= query_pos)
        bias[...] = jnp.where(allowed, 0.0, -1e30)

    def store_own(cols, value):
        dkv_own[:, cols] = value

    set_bias(own)
    tile(lambda cols: kv_own[:, cols], True, True, store_own)

    def visit(step, _):
        block = own ^ step

        @pl.when(block < own)
        def _():
            slot = step - 1
            pltpu.make_async_copy(kv_buf.at[slot], kv_buf.at[slot], in_sem.at[slot]).wait()
            end = (base + block + 1) * rows
            needed = first_start < end
            full = last_start <= (base + block) * rows

            def store(cols, value):
                dkv_buf[slot, :, cols] = value.astype(dkv_buf.dtype)

            def load(cols):
                return kv_buf[slot, :, cols]

            @pl.when(full)
            def _():
                tile(load, False, False, store)

            @pl.when(needed & jnp.logical_not(full))
            def _():
                set_bias(block)
                tile(load, True, False, store)

            @pl.when(jnp.logical_not(needed))
            def _():
                dkv_buf[slot] = jnp.zeros(dkv_buf.shape[1:], dkv_buf.dtype)

        return 0

    lax.fori_loop(1, half, visit, 0)
    for step in range(1, half):
        @pl.when((own ^ step) < own)
        def _():
            pltpu.make_async_copy(dkv_buf.at[step - 1], dkv_out[step - 1], out_sem.at[step - 1]).start()
    dq_ref[...] = (dq_acc[...] * SCORE_SCALE).astype(dq_ref.dtype)
    for step in range(1, half):
        @pl.when((own ^ step) < own)
        def _():
            pltpu.make_async_copy(dkv_buf.at[step - 1], dkv_out[step - 1], out_sem.at[step - 1]).wait()


def attention_grads(info, start, q_rows, out_grad, lse2, delta, kv_own, kv_in, kv_heads):
    half = len(kv_in) + 1
    rows, width = q_rows.shape
    group = width // (DH * kv_heads)
    any_spec = pl.BlockSpec(memory_space=pl.ANY)
    vmem_spec = pl.BlockSpec(memory_space=pltpu.VMEM)
    kv_shape = kv_own.shape

    def kernel(info_ref, *refs):
        grads_kernel(half, kv_heads, group, info_ref, *refs)

    tiles = half
    return pl.pallas_call(
        kernel,
        out_shape=[
            jax.ShapeDtypeStruct((rows, width), jnp.bfloat16),
            jax.ShapeDtypeStruct(kv_shape, jnp.float32),
        ]
        + [jax.ShapeDtypeStruct(kv_shape, jnp.bfloat16)] * (half - 1),
        in_specs=[pl.BlockSpec(memory_space=pltpu.SMEM)] + [vmem_spec] * 6 + [any_spec] * (half - 1),
        out_specs=[vmem_spec] * 2 + [any_spec] * (half - 1),
        scratch_shapes=[
            pltpu.VMEM((half - 1,) + kv_shape, jnp.bfloat16),
            pltpu.VMEM((half - 1,) + kv_shape, jnp.bfloat16),
            pltpu.VMEM((rows, width), jnp.float32),
            pltpu.VMEM((rows, DH), jnp.float32),
            pltpu.VMEM((rows, DH), jnp.float32),
            pltpu.VMEM((rows, rows), jnp.float32),
            pltpu.SemaphoreType.DMA((half - 1,)),
            pltpu.SemaphoreType.DMA((half - 1,)),
        ],
        compiler_params=pltpu.CompilerParams(vmem_limit_bytes=56 << 20),
        cost_estimate=pl.CostEstimate(
            flops=10 * rows * rows * width * tiles,
            bytes_accessed=8 * rows * width + 8 * tiles * rows * kv_shape[1],
            transcendentals=rows * rows * (width // DH) * tiles,
        ),
        name="attention_grads",
    )(info, start, q_rows, out_grad, lse2, delta, kv_own, *kv_in)


def per_device(queries, keys, values, attn_out, out_grad, log_sum, file_ids):
    ctx_count = lax.axis_size("ctx")
    head_count = lax.axis_size("head")
    half = ctx_count // 2
    index = lax.axis_index("ctx")
    own = index % half
    base = index - own
    part_rows = queries.shape[0]
    rows = out_grad.shape[0]
    heads = log_sum.shape[0]
    kv_width = keys.shape[1] // head_count
    kv_heads = kv_width // DH

    def to_heads(x):
        return lax.all_to_all(x, "head", split_axis=0, concat_axis=0, tiled=True)

    def by_head(x):
        return x.reshape(part_rows, head_count, -1).transpose(1, 0, 2)

    all_ids = lax.all_gather(file_ids, "ctx", axis=0, tiled=True)
    kv_send = jnp.concatenate([by_head(keys), by_head(values)], axis=2)
    kv_own = to_heads(kv_send.reshape(rows, 2 * kv_width))
    q_rows = to_heads(by_head(queries).reshape(rows, heads * DH))
    delta = row_deltas(out_grad, attn_out, heads)

    def forward_route(step):
        pairs = []
        for i in range(ctx_count):
            j = (i // half) * half + ((i % half) ^ step)
            if i < j:
                pairs.append((i, j))
        return pairs

    kv_in = [lax.ppermute(kv_own, "ctx", forward_route(step)) for step in range(1, half)]
    start = jnp.sum(
        (all_ids[None, :] < file_ids[:, None]).astype(jnp.int32), axis=1, dtype=jnp.int32
    )
    info = jnp.stack([own, start[0], start[-1], base]).astype(jnp.int32)
    dq, dkv_own, *dkv_parts = attention_grads(
        info, start[None, :], q_rows, out_grad, log_sum * LOG2E, delta, kv_own, kv_in, kv_heads
    )
    q_back = lax.all_to_all(dq, "head", split_axis=0, concat_axis=0, tiled=True)
    dkv = dkv_own
    for step in range(1, half):
        back = [(j, i) for i, j in forward_route(step)]
        dkv = dkv + lax.ppermute(dkv_parts[step - 1], "ctx", back).astype(jnp.float32)
    kv_back = to_heads(dkv.astype(jnp.bfloat16)).reshape(head_count, part_rows, 2, kv_width)

    def joined(x):
        return x.transpose(1, 0, 2).reshape(part_rows, -1)

    q_grad = joined(q_back.reshape(head_count, part_rows, -1))
    return (q_grad, joined(kv_back[:, :, 0]), joined(kv_back[:, :, 1]))


def solution(mesh):
    return jax.shard_map(
        per_device,
        mesh=mesh,
        in_specs=(
            P(("ctx", "head"), None),
            P(("ctx", "head"), None),
            P(("ctx", "head"), None),
            P("ctx", "head"),
            P("ctx", "head"),
            P("head", "ctx"),
            P("ctx"),
        ),
        out_specs=(P(("ctx", "head"), None), P(("ctx", "head"), None), P(("ctx", "head"), None)),
        check_vma=False,
    )
```

```python
import math

import jax
import jax.numpy as jnp
from jax import lax
from jax.experimental import pallas as pl
from jax.experimental.pallas import tpu as pltpu
from jax.sharding import PartitionSpec as P

DH = 128
TAG_ROWS = 16
SCORE_SCALE = 1.0 / math.sqrt(DH)
LOG2E = math.log2(math.e)
NT = (((1,), (1,)), ((), ()))
NN = (((1,), (0,)), ((), ()))
TN = (((0,), (0,)), ((), ()))
ANY = pl.BlockSpec(memory_space=pl.ANY)
VMEM = pl.BlockSpec(memory_space=pltpu.VMEM)


def dot(a, b, dims):
    return lax.dot_general(a, b, dims, preferred_element_type=jnp.float32)


def aligned(index, size):
    return pl.ds(pl.multiple_of(index * size, size), size)


def run_copies(pairs, sems):
    copies = [pltpu.make_async_copy(src, dst, sems.at[i]) for i, (src, dst) in enumerate(pairs)]
    for copy in copies:
        copy.start()
    for copy in copies:
        copy.wait()


def cost(flops, moved):
    return pl.CostEstimate(flops=flops, bytes_accessed=moved, transcendentals=0)


def row_deltas(out_grad, attn_out, heads):
    rows = out_grad.shape[0]

    def kernel(grad_ref, out_ref, delta_ref):
        for head in range(heads):
            cols = slice(head * DH, (head + 1) * DH)
            prod = grad_ref[:, cols].astype(jnp.float32) * out_ref[:, cols].astype(jnp.float32)
            delta_ref[head : head + 1, :] = jnp.sum(jnp.transpose(prod), axis=0, keepdims=True)

    return pl.pallas_call(
        kernel,
        out_shape=jax.ShapeDtypeStruct((heads, rows), jnp.float32),
        compiler_params=pltpu.CompilerParams(vmem_limit_bytes=32 << 20),
        cost_estimate=cost(4 * rows * heads * DH, 4 * rows * heads * DH),
        name="row_deltas",
    )(out_grad, attn_out)


def pack_kv(keys, values, head_count):
    part, width = keys.shape[0], keys.shape[1] // head_count

    def kernel(k_ref, v_ref, *refs):
        outs, sems = refs[:-1], refs[-1]
        own = lax.axis_index("head")
        pairs = []
        for step in range(1, head_count):
            cols = aligned(own ^ step, width)
            pairs.append((k_ref.at[:, cols], outs[step - 1].at[:, :width]))
            pairs.append((v_ref.at[:, cols], outs[step - 1].at[:, width:]))
        run_copies(pairs, sems)

    return pl.pallas_call(
        kernel,
        out_shape=[jax.ShapeDtypeStruct((part, 2 * width), keys.dtype)] * (head_count - 1),
        in_specs=[ANY] * 2,
        out_specs=[ANY] * (head_count - 1),
        scratch_shapes=[pltpu.SemaphoreType.DMA((2 * (head_count - 1),))],
        cost_estimate=cost(0, 4 * part * keys.shape[1]),
        name="pack_kv",
    )(keys, values)


def pack_q(queries, head_count, chunks):
    part, width = queries.shape[0], queries.shape[1] // (head_count * chunks)

    def kernel(q_ref, *refs):
        outs, sems = refs[:-1], refs[-1]
        own = lax.axis_index("head")
        pairs = []
        for chunk in range(chunks):
            for step in range(1, head_count):
                cols = aligned((own ^ step) * chunks + chunk, width)
                pairs.append((q_ref.at[:, cols], outs[chunk * (head_count - 1) + step - 1]))
        run_copies(pairs, sems)

    count = chunks * (head_count - 1)
    return pl.pallas_call(
        kernel,
        out_shape=[jax.ShapeDtypeStruct((part, width), queries.dtype)] * count,
        in_specs=[ANY],
        out_specs=[ANY] * count,
        scratch_shapes=[pltpu.SemaphoreType.DMA((count,))],
        cost_estimate=cost(0, 4 * part * queries.shape[1]),
        name="pack_q",
    )(queries)


def join_kv(keys, values, parts, tags):
    head_count = len(parts) + 1
    part, width = keys.shape[0], keys.shape[1] // head_count
    rows = part * head_count

    def kernel(k_ref, v_ref, tag_ref, *refs):
        ins, out, sems = refs[: head_count - 1], refs[-2], refs[-1]
        own = lax.axis_index("head")
        pairs = [
            (k_ref.at[:, aligned(own, width)], out.at[aligned(own, part), :width]),
            (v_ref.at[:, aligned(own, width)], out.at[aligned(own, part), width:]),
            (tag_ref, out.at[rows:]),
        ]
        for step in range(1, head_count):
            pairs.append((ins[step - 1], out.at[aligned(own ^ step, part)]))
        run_copies(pairs, sems)

    return pl.pallas_call(
        kernel,
        out_shape=jax.ShapeDtypeStruct((rows + tags.shape[0], 2 * width), keys.dtype),
        in_specs=[ANY] * (2 + head_count),
        out_specs=ANY,
        scratch_shapes=[pltpu.SemaphoreType.DMA((head_count + 2,))],
        cost_estimate=cost(0, 8 * rows * width),
        name="join_kv",
    )(keys, values, tags, *parts)


def chunk_grads(chunk, chunks, half, queries, q_parts, out_grad, log_sum, delta, kv_own, kv_in):
    head_count = len(q_parts) + 1
    part, width = q_parts[0].shape
    rows = part * head_count
    group = width // DH
    slots = half

    def kernel(*refs):
        lse_ref, delta_ref, q_own, g_in = refs[:4]
        q_in = refs[4 : 3 + head_count]
        kv_refs = refs[3 + head_count : 3 + head_count + slots]
        outs = refs[3 + head_count + slots :]
        dq_out = outs[:head_count]
        own_out = outs[head_count]
        dkv_out = outs[head_count + 1 : head_count + slots]
        (q_buf, g_buf, kv_buf, tag_buf, dkv_buf, dq_acc, dq_low, dk_acc, dv_acc, bias) = outs[
            head_count + slots : -3
        ]
        in_sem, kv_sem, out_sem = outs[-3:]
        head_index = lax.axis_index("head")
        own = lax.rem(lax.axis_index("ctx"), half)
        loads = [
            (q_own.at[:, aligned(head_index * chunks + chunk, width)], q_buf.at[aligned(head_index, part)])
        ]
        for step in range(1, head_count):
            loads.append((q_in[step - 1], q_buf.at[aligned(head_index ^ step, part)]))
        loads.append((g_in.at[:, chunk * width : (chunk + 1) * width], g_buf))
        loads = [pltpu.make_async_copy(s, d, in_sem.at[i]) for i, (s, d) in enumerate(loads)]

        def kv_copies(slot):
            src = kv_refs[slot]
            k_cols = slice(chunk * DH, (chunk + 1) * DH)
            v_cols = slice((chunks + chunk) * DH, (chunks + chunk + 1) * DH)
            return [
                pltpu.make_async_copy(src.at[:rows, k_cols], kv_buf.at[slot, :, :DH], kv_sem.at[slot, 0]),
                pltpu.make_async_copy(src.at[:rows, v_cols], kv_buf.at[slot, :, DH:], kv_sem.at[slot, 1]),
                pltpu.make_async_copy(src.at[rows:], tag_buf.at[slot], kv_sem.at[slot, 2]),
            ]

        for slot in range(slots):
            if slot == 0:
                for copy in kv_copies(slot) + loads:
                    copy.start()
            else:
                @pl.when((own ^ slot) < own)
                def _():
                    for copy in kv_copies(slot):
                        copy.start()

        dq_acc[...] = jnp.zeros_like(dq_acc)
        for copy in kv_copies(0) + loads:
            copy.wait()

        def load_tags(slot):
            pieces = []
            for first in range(0, rows, tag_buf.shape[2]):
                row = first // tag_buf.shape[2] * TAG_ROWS
                size = min(rows - first, tag_buf.shape[2])
                pieces.append(tag_buf[slot, row : row + TAG_ROWS, :size].astype(jnp.float32)[:8])
            return pieces[0] if len(pieces) == 1 else jnp.concatenate(pieces, axis=1)

        own_tags = load_tags(0)
        own_low, own_high = jnp.min(own_tags), jnp.max(own_tags)

        def tile(slot, masked):
            key = kv_buf[slot, :, :DH]
            value = kv_buf[slot, :, DH:]
            for member in range(group):
                head = chunk * group + member
                cols = slice(member * DH, (member + 1) * DH)
                query = q_buf[:, cols]
                grad = g_buf[:, cols]
                lse = lse_ref[head : head + 1, :] * LOG2E
                scores = dot(key, query, NT) * (SCORE_SCALE * LOG2E) - lse
                if masked:
                    scores = scores + bias[...]
                probs = jnp.exp2(scores)
                dprobs = dot(value, grad, NT)
                dscores = (probs * (dprobs - delta_ref[head : head + 1, :])).astype(jnp.bfloat16)
                dv_part = dot(probs.astype(jnp.bfloat16), grad, NN)
                dk_part = dot(dscores, query, NN)
                dq_part = dot(dscores, key, TN)
                if member == 0:
                    dv_acc[...] = dv_part
                    dk_acc[...] = dk_part
                else:
                    dv_acc[...] += dv_part
                    dk_acc[...] += dk_part
                dq_acc[:, cols] += dq_part

        def store(slot):
            dk = dk_acc[...] * SCORE_SCALE
            dv = dv_acc[...]

            @pl.when(slot == 0)
            def _():
                own_out[:, :DH] = dk
                own_out[:, DH:] = dv

            @pl.when(slot > 0)
            def _():
                dkv_buf[slot, :, :DH] = dk.astype(jnp.bfloat16)
                dkv_buf[slot, :, DH:] = dv.astype(jnp.bfloat16)

        def visit(slot, _):
            block = own ^ slot

            @pl.when(block <= own)
            def _():
                @pl.when(slot > 0)
                def _():
                    pltpu.make_async_copy(
                        kv_buf.at[slot, :, :DH], kv_buf.at[slot, :, :DH], kv_sem.at[slot, 0]
                    ).wait()
                    pltpu.make_async_copy(
                        kv_buf.at[slot, :, DH:], kv_buf.at[slot, :, DH:], kv_sem.at[slot, 1]
                    ).wait()
                    pltpu.make_async_copy(tag_buf.at[slot], tag_buf.at[slot], kv_sem.at[slot, 2]).wait()

                tags = load_tags(slot)
                needed = jnp.max(tags) == own_low
                full = (jnp.min(tags) == own_high) & (slot > 0)

                @pl.when(full)
                def _():
                    tile(slot, False)
                    store(slot)

                @pl.when(jnp.logical_not(full) & (needed | (slot == 0)))
                def _():
                    key_tags = jnp.transpose(tags)[:, :1]
                    key_pos = block * rows + lax.broadcasted_iota(jnp.int32, (rows, rows), 0)
                    query_pos = own * rows + lax.broadcasted_iota(jnp.int32, (rows, rows), 1)
                    allowed = (key_tags == own_tags[:1, :]) & (key_pos <= query_pos)
                    bias[...] = jnp.where(allowed, 0.0, -1e30)
                    tile(slot, True)
                    store(slot)

                @pl.when(jnp.logical_not(full | needed | (slot == 0)))
                def _():
                    dkv_buf[slot] = jnp.zeros(dkv_buf.shape[1:], dkv_buf.dtype)

            return 0

        lax.fori_loop(0, slots, visit, 0)

        def dkv_copy(slot):
            return pltpu.make_async_copy(dkv_buf.at[slot], dkv_out[slot - 1], out_sem.at[slot])

        for slot in range(1, slots):
            @pl.when((own ^ slot) < own)
            def _():
                dkv_copy(slot).start()
        dq_low[...] = (dq_acc[...] * SCORE_SCALE).astype(dq_low.dtype)
        sends = [
            pltpu.make_async_copy(
                dq_low.at[aligned(head_index ^ step, part)], dq_out[step], in_sem.at[step]
            )
            for step in range(head_count)
        ]
        for copy in sends:
            copy.start()
        for copy in sends:
            copy.wait()
        for slot in range(1, slots):
            @pl.when((own ^ slot) < own)
            def _():
                dkv_copy(slot).wait()

    bf16, f32 = jnp.bfloat16, jnp.float32
    heads = log_sum.shape[0]
    return pl.pallas_call(
        kernel,
        out_shape=[jax.ShapeDtypeStruct((part, width), bf16)] * head_count
        + [jax.ShapeDtypeStruct((rows, 2 * DH), f32)]
        + [jax.ShapeDtypeStruct((rows, 2 * DH), bf16)] * (slots - 1),
        in_specs=[VMEM] * 2 + [ANY] * (1 + head_count + slots),
        out_specs=[ANY] * head_count + [VMEM] + [ANY] * (slots - 1),
        scratch_shapes=[
            pltpu.VMEM((rows, width), bf16),
            pltpu.VMEM((rows, width), bf16),
            pltpu.VMEM((slots, rows, 2 * DH), bf16),
            pltpu.VMEM((slots, kv_own.shape[0] - rows, kv_own.shape[1]), bf16),
            pltpu.VMEM((slots, rows, 2 * DH), bf16),
            pltpu.VMEM((rows, width), f32),
            pltpu.VMEM((rows, width), bf16),
            pltpu.VMEM((rows, DH), f32),
            pltpu.VMEM((rows, DH), f32),
            pltpu.VMEM((rows, rows), f32),
            pltpu.SemaphoreType.DMA((head_count + 1,)),
            pltpu.SemaphoreType.DMA((slots, 3)),
            pltpu.SemaphoreType.DMA((slots,)),
        ],
        compiler_params=pltpu.CompilerParams(vmem_limit_bytes=48 << 20),
        cost_estimate=pl.CostEstimate(
            flops=10 * rows * rows * width * slots,
            bytes_accessed=8 * rows * width + 8 * slots * rows * 2 * DH,
            transcendentals=rows * rows * group * slots,
        ),
        name="chunk_grads",
    )(log_sum, delta, queries, out_grad, *q_parts, kv_own, *kv_in)


def sum_kv(own_part, parts, head_count):
    rows, width = own_part.shape
    part = rows // head_count

    def kernel(own_ref, *refs):
        ins, outs, total = refs[: len(parts)], refs[len(parts) : -1], refs[-1]
        value = own_ref[...]
        for ref in ins:
            value = value + ref[...].astype(jnp.float32)
        total[...] = value.astype(jnp.bfloat16)
        index = lax.axis_index("head")
        for step in range(head_count):
            outs[step][...] = total[aligned(index ^ step, part), :]

    return pl.pallas_call(
        kernel,
        out_shape=[jax.ShapeDtypeStruct((part, width), jnp.bfloat16)] * head_count,
        scratch_shapes=[pltpu.VMEM((rows, width), jnp.bfloat16)],
        compiler_params=pltpu.CompilerParams(vmem_limit_bytes=32 << 20),
        cost_estimate=cost(4 * rows * width, 12 * rows * width),
        name="sum_kv",
    )(own_part, *parts)


def join_grads(dq_parts, dkv_parts):
    chunks, head_count = len(dq_parts), len(dq_parts[0])
    part, width = dq_parts[0][0].shape
    count = chunks * head_count

    def kernel(*refs):
        q_ins, kv_ins = refs[:count], refs[count : 2 * count]
        q_out, k_out, v_out, sems = refs[2 * count :]
        own = lax.axis_index("head")
        pairs = []
        for chunk in range(chunks):
            for step in range(head_count):
                slot = (own ^ step) * chunks + chunk
                q_ref = q_ins[chunk * head_count + step]
                kv_ref = kv_ins[chunk * head_count + step]
                pairs.append((q_ref, q_out.at[:, aligned(slot, width)]))
                pairs.append((kv_ref.at[:, :DH], k_out.at[:, aligned(slot, DH)]))
                pairs.append((kv_ref.at[:, DH:], v_out.at[:, aligned(slot, DH)]))
        run_copies(pairs, sems)

    kv_shape = jax.ShapeDtypeStruct((part, count * DH), jnp.bfloat16)
    return pl.pallas_call(
        kernel,
        out_shape=[jax.ShapeDtypeStruct((part, count * width), jnp.bfloat16), kv_shape, kv_shape],
        in_specs=[ANY] * (2 * count),
        out_specs=[ANY] * 3,
        scratch_shapes=[pltpu.SemaphoreType.DMA((3 * count,))],
        cost_estimate=cost(0, 5 * part * count * width),
        name="join_grads",
    )(*[x for group in dq_parts for x in group], *[x for group in dkv_parts for x in group])


def per_device(queries, keys, values, attn_out, out_grad, log_sum, file_ids):
    ctx_count = lax.axis_size("ctx")
    head_count = lax.axis_size("head")
    half = ctx_count // 2
    rows = out_grad.shape[0]
    heads = log_sum.shape[0]
    kv_width = keys.shape[1] // head_count
    chunks = kv_width // DH

    def over_head(blocks):
        return [
            lax.ppermute(x, "head", [(i, i ^ step) for i in range(head_count)])
            for step, x in enumerate(blocks, 1)
        ]

    def route(step):
        pairs = [(i, i - i % half + (i % half ^ step)) for i in range(ctx_count)]
        return [(i, j) for i, j in pairs if i < j]

    tag_groups = pl.cdiv(rows, 2 * kv_width)
    tags = jnp.pad(file_ids.astype(jnp.bfloat16), (0, tag_groups * 2 * kv_width - rows))
    tags = jnp.repeat(tags.reshape(tag_groups, 2 * kv_width), TAG_ROWS, axis=0)
    kv_parts = over_head(pack_kv(keys, values, head_count))
    q_packed = pack_q(queries, head_count, chunks)
    steps = head_count - 1
    q_parts = [over_head(q_packed[i * steps : (i + 1) * steps]) for i in range(chunks)]
    kv_own = join_kv(keys, values, kv_parts, tags)
    delta = row_deltas(out_grad, attn_out, heads)
    kv_in = [lax.ppermute(kv_own, "ctx", route(step)) for step in range(1, half)]

    dq_parts, dkv_parts = [], []
    for chunk in range(chunks):
        outs = chunk_grads(
            chunk, chunks, half, queries, q_parts[chunk], out_grad, log_sum, delta, kv_own, kv_in
        )
        dq_parts.append([outs[0]] + over_head(outs[1:head_count]))
        back = [
            lax.ppermute(x, "ctx", [(j, i) for i, j in route(step)])
            for step, x in enumerate(outs[head_count + 1 :], 1)
        ]
        pieces = sum_kv(outs[head_count], back, head_count)
        dkv_parts.append([pieces[0]] + over_head(pieces[1:]))
    return tuple(join_grads(dq_parts, dkv_parts))


def solution(mesh):
    return jax.shard_map(
        per_device,
        mesh=mesh,
        in_specs=(
            P(("ctx", "head"), None),
            P(("ctx", "head"), None),
            P(("ctx", "head"), None),
            P("ctx", "head"),
            P("ctx", "head"),
            P("head", "ctx"),
            P("ctx"),
        ),
        out_specs=(P(("ctx", "head"), None), P(("ctx", "head"), None), P(("ctx", "head"), None)),
        check_vma=False,
    )
```

```python
import math

import jax
import jax.numpy as jnp
from jax import lax
from jax.experimental import pallas as pl
from jax.experimental.pallas import tpu as pltpu
from jax.sharding import PartitionSpec as P

DH = 128
TAG_ROWS = 16
SCORE_SCALE = 1.0 / math.sqrt(DH)
LOG2E = math.log2(math.e)
NT = (((1,), (1,)), ((), ()))
NN = (((1,), (0,)), ((), ()))
TN = (((0,), (0,)), ((), ()))
ANY = pl.BlockSpec(memory_space=pl.ANY)
VMEM = pl.BlockSpec(memory_space=pltpu.VMEM)


def dot(a, b, dims):
    return lax.dot_general(a, b, dims, preferred_element_type=jnp.float32)


def aligned(index, size):
    return pl.ds(pl.multiple_of(index * size, size), size)


def cost(flops, moved):
    return pl.CostEstimate(flops=flops, bytes_accessed=moved, transcendentals=0)


def row_deltas(out_grad, attn_out, heads):
    rows = out_grad.shape[0]

    def kernel(grad_ref, out_ref, delta_ref):
        for head in range(heads):
            cols = slice(head * DH, (head + 1) * DH)
            prod = grad_ref[:, cols].astype(jnp.float32) * out_ref[:, cols].astype(jnp.float32)
            delta_ref[head : head + 1, :] = jnp.sum(jnp.transpose(prod), axis=0, keepdims=True)

    return pl.pallas_call(
        kernel,
        out_shape=jax.ShapeDtypeStruct((heads, rows), jnp.float32),
        compiler_params=pltpu.CompilerParams(vmem_limit_bytes=32 << 20),
        cost_estimate=cost(4 * rows * heads * DH, 4 * rows * heads * DH),
        name="row_deltas",
    )(out_grad, attn_out)


def pack_kv(keys, values, head_count, chunks):
    part = keys.shape[0]

    def kernel(k_ref, v_ref, *outs):
        own = lax.axis_index("head")
        for step in range(head_count):
            for chunk in range(chunks):
                cols = aligned((own ^ step) * chunks + chunk, DH)
                at = 2 * DH * chunk
                outs[step][:, at : at + DH] = k_ref[:, cols]
                outs[step][:, at + DH : at + 2 * DH] = v_ref[:, cols]

    return pl.pallas_call(
        kernel,
        out_shape=[jax.ShapeDtypeStruct((part, 2 * chunks * DH), keys.dtype)] * head_count,
        cost_estimate=cost(0, 8 * keys.size),
        name="pack_kv",
    )(keys, values)


def pack_q(queries, head_count, chunks, whole):
    part, width = queries.shape[0], queries.shape[1] // (head_count * chunks)
    layout = []
    for step in range(head_count):
        layout += [(step, 0, chunks)] if step in whole else [(step, c, 1) for c in range(chunks)]

    def kernel(q_ref, *outs):
        own = lax.axis_index("head")
        for out, (step, chunk, count) in zip(outs, layout):
            first = pl.multiple_of(((own ^ step) * chunks + chunk) * width, width)
            out[...] = q_ref[:, pl.ds(first, count * width)]

    outs = pl.pallas_call(
        kernel,
        out_shape=[
            jax.ShapeDtypeStruct((part, count * width), queries.dtype) for _, _, count in layout
        ],
        compiler_params=pltpu.CompilerParams(vmem_limit_bytes=32 << 20),
        cost_estimate=cost(0, 4 * queries.size),
        name="pack_q",
    )(queries)
    return {(step, chunk): out for out, (step, chunk, _) in zip(outs, layout)}


def join_kv(parts, file_ids, chunks):
    head_count = len(parts)
    part, width = parts[0].shape[0], 2 * DH
    rows = part * head_count
    tag_lines = pl.cdiv(rows, width)

    def kernel(tag_ref, *refs):
        ins, outs = refs[:head_count], refs[head_count:]
        own = lax.axis_index("head")
        line = lax.broadcasted_iota(jnp.int32, (TAG_ROWS, DH), 0)
        tags = tag_ref[...].astype(jnp.float32)
        for chunk, out in enumerate(outs):
            for step in range(head_count):
                out[aligned(own ^ step, part), :] = ins[step][:, chunk * width : (chunk + 1) * width]
            for column in range(0, width, DH):
                value = jnp.zeros((TAG_ROWS, DH), jnp.float32)
                for index in range(tag_lines):
                    first = index * width + column
                    if first < rows:
                        value = jnp.where(line == index, tags[:, first : first + DH], value)
                out[rows:, column : column + DH] = value.astype(out.dtype)

    shape = jax.ShapeDtypeStruct((rows + TAG_ROWS, width), parts[0].dtype)
    return pl.pallas_call(
        kernel,
        out_shape=[shape] * chunks,
        cost_estimate=cost(0, 4 * rows * width * chunks),
        name="join_kv",
    )(file_ids[None, :], *parts)


def chunk_grads(chunk, half, q_parts, out_grad, log_sum, delta, kv_blocks):
    head_count = len(q_parts)
    part, rows = q_parts[0].shape[0], out_grad.shape[0]
    width = min(x.shape[1] for x in q_parts)
    group = width // DH
    pair = 2 if group % 2 == 0 else 1
    slots = half

    def kernel(*refs):
        lse_ref, delta_ref, g_in = refs[:3]
        q_in = refs[3 : 3 + head_count]
        kv_refs = refs[3 + head_count : 3 + head_count + slots]
        outs = refs[3 + head_count + slots :]
        dq_out = outs[:head_count]
        own_out = outs[head_count]
        dkv_out = outs[head_count + 1 : head_count + slots]
        (q_buf, g_buf, kv_buf, dkv_buf, dq_acc, dq_low, dk_acc, dv_acc, bias) = outs[
            head_count + slots : -3
        ]
        in_sem, kv_sem, out_sem = outs[-3:]
        head_index = lax.axis_index("head")
        own = lax.rem(lax.axis_index("ctx"), half)
        loads = [
            (
                ref if ref.shape[1] == width else ref.at[:, chunk * width : (chunk + 1) * width],
                q_buf.at[aligned(head_index ^ step, part)],
            )
            for step, ref in enumerate(q_in)
        ]
        loads.append((g_in.at[:, chunk * width : (chunk + 1) * width], g_buf))
        loads = [pltpu.make_async_copy(s, d, in_sem.at[i]) for i, (s, d) in enumerate(loads)]

        def kv_copy(slot):
            return pltpu.make_async_copy(kv_refs[slot], kv_buf.at[slot], kv_sem.at[slot])

        for slot in range(slots):
            if slot == 0:
                for copy in [kv_copy(slot)] + loads:
                    copy.start()
            else:
                @pl.when((own ^ slot) < own)
                def _():
                    kv_copy(slot).start()

        dq_acc[...] = jnp.zeros_like(dq_acc)
        for copy in [kv_copy(0)] + loads:
            copy.wait()

        def load_tags(slot):
            lines = kv_buf[slot, rows:, :].astype(jnp.float32)
            pieces = [
                lines[first // (2 * DH) : first // (2 * DH) + 1, : min(rows - first, 2 * DH)]
                for first in range(0, rows, 2 * DH)
            ]
            return jnp.concatenate(pieces, axis=1)

        own_tags = load_tags(0)
        own_low, own_high = jnp.min(own_tags), jnp.max(own_tags)

        def tile(slot, masked):
            key = kv_buf[slot, :rows, :DH]
            value = kv_buf[slot, :rows, DH:]
            for first in range(0, group, pair):
                heads_here = [chunk * group + first + i for i in range(pair)]
                columns = [slice((first + i) * DH, (first + i + 1) * DH) for i in range(pair)]
                query = jnp.concatenate([q_buf[:, cols] for cols in columns], axis=0)
                grad = jnp.concatenate([g_buf[:, cols] for cols in columns], axis=0)
                lse = jnp.concatenate([lse_ref[h : h + 1, :] for h in heads_here], axis=1) * LOG2E
                shift = jnp.concatenate([delta_ref[h : h + 1, :] for h in heads_here], axis=1)
                scores = dot(key, query, NT) * (SCORE_SCALE * LOG2E) - lse
                if masked:
                    scores = scores + jnp.concatenate([bias[...]] * pair, axis=1)
                probs = jnp.exp2(scores)
                dprobs = dot(value, grad, NT)
                dscores = (probs * (dprobs - shift)).astype(jnp.bfloat16)
                dv_part = dot(probs.astype(jnp.bfloat16), grad, NN)
                dk_part = dot(dscores, query, NN)
                dq_part = dot(key, dscores, TN)
                if first == 0:
                    dv_acc[...] = dv_part
                    dk_acc[...] = dk_part
                else:
                    dv_acc[...] += dv_part
                    dk_acc[...] += dk_part
                for i in range(pair):
                    dq_acc[columns[i], :] += dq_part[:, i * rows : (i + 1) * rows]

        def store(slot):
            dk = dk_acc[...] * SCORE_SCALE
            dv = dv_acc[...]

            @pl.when(slot == 0)
            def _():
                own_out[:, :DH] = dk
                own_out[:, DH:] = dv

            @pl.when(slot > 0)
            def _():
                dkv_buf[slot, :, :DH] = dk.astype(jnp.bfloat16)
                dkv_buf[slot, :, DH:] = dv.astype(jnp.bfloat16)

        def visit(slot, _):
            block = own ^ slot

            @pl.when(block <= own)
            def _():
                @pl.when(slot > 0)
                def _():
                    pltpu.make_async_copy(kv_buf.at[slot], kv_buf.at[slot], kv_sem.at[slot]).wait()

                tags = load_tags(slot)
                needed = jnp.max(tags) == own_low
                full = (jnp.min(tags) == own_high) & (slot > 0)

                @pl.when(full)
                def _():
                    tile(slot, False)
                    store(slot)

                @pl.when(jnp.logical_not(full) & (needed | (slot == 0)))
                def _():
                    key_tags = jnp.transpose(jnp.broadcast_to(tags, (8, rows)))[:, :1]
                    key_pos = block * rows + lax.broadcasted_iota(jnp.int32, (rows, rows), 0)
                    query_pos = own * rows + lax.broadcasted_iota(jnp.int32, (rows, rows), 1)
                    allowed = (key_tags == own_tags) & (key_pos <= query_pos)
                    bias[...] = jnp.where(allowed, 0.0, -1e30)
                    tile(slot, True)
                    store(slot)

                @pl.when(jnp.logical_not(full | needed | (slot == 0)))
                def _():
                    dkv_buf[slot] = jnp.zeros(dkv_buf.shape[1:], dkv_buf.dtype)

            return 0

        lax.fori_loop(0, slots, visit, 0)

        def dkv_copy(slot):
            return pltpu.make_async_copy(dkv_buf.at[slot], dkv_out[slot - 1], out_sem.at[slot])

        for slot in range(1, slots):
            @pl.when((own ^ slot) < own)
            def _():
                dkv_copy(slot).start()
        for member in range(group):
            cols = slice(member * DH, (member + 1) * DH)
            dq_low[:, cols] = jnp.transpose((dq_acc[cols, :] * SCORE_SCALE).astype(dq_low.dtype))
        sends = [
            pltpu.make_async_copy(
                dq_low.at[aligned(head_index ^ step, part)], dq_out[step], in_sem.at[step]
            )
            for step in range(head_count)
        ]
        for copy in sends:
            copy.start()
        for copy in sends:
            copy.wait()
        for slot in range(1, slots):
            @pl.when((own ^ slot) < own)
            def _():
                dkv_copy(slot).wait()

    bf16, f32 = jnp.bfloat16, jnp.float32
    heads = log_sum.shape[0]
    return pl.pallas_call(
        kernel,
        out_shape=[jax.ShapeDtypeStruct((part, width), bf16)] * head_count
        + [jax.ShapeDtypeStruct((rows, 2 * DH), f32)]
        + [jax.ShapeDtypeStruct((rows, 2 * DH), bf16)] * (slots - 1),
        in_specs=[VMEM] * 2 + [ANY] * (1 + head_count + slots),
        out_specs=[ANY] * head_count + [VMEM] + [ANY] * (slots - 1),
        scratch_shapes=[
            pltpu.VMEM((rows, width), bf16),
            pltpu.VMEM((rows, width), bf16),
            pltpu.VMEM((slots,) + kv_blocks[0].shape, bf16),
            pltpu.VMEM((slots, rows, 2 * DH), bf16),
            pltpu.VMEM((width, rows), f32),
            pltpu.VMEM((rows, width), bf16),
            pltpu.VMEM((rows, DH), f32),
            pltpu.VMEM((rows, DH), f32),
            pltpu.VMEM((rows, rows), f32),
            pltpu.SemaphoreType.DMA((head_count + 1,)),
            pltpu.SemaphoreType.DMA((slots,)),
            pltpu.SemaphoreType.DMA((slots,)),
        ],
        compiler_params=pltpu.CompilerParams(vmem_limit_bytes=48 << 20),
        cost_estimate=pl.CostEstimate(
            flops=10 * rows * rows * width * slots,
            bytes_accessed=8 * rows * width + 8 * slots * rows * 2 * DH,
            transcendentals=rows * rows * group * slots,
        ),
        name="chunk_grads",
    )(log_sum, delta, out_grad, *q_parts, *kv_blocks)


def sum_kv(parts, head_count, half):
    chunks, count = len(parts), len(parts[0])
    rows, width = parts[0][0].shape
    part = rows // head_count

    def kernel(*refs):
        ins, outs, total = refs[: chunks * count], refs[chunks * count : -1], refs[-1]
        block = lax.rem(lax.axis_index("ctx"), half)
        for chunk in range(chunks):
            value = ins[chunk * count][...]
            for step in range(1, count):
                later = jnp.full((1, width), block ^ step, jnp.int32) > block
                sent = ins[chunk * count + step][...].astype(jnp.float32)
                value = value + jnp.where(later, sent, 0.0)
            total[:, chunk * width : (chunk + 1) * width] = value.astype(jnp.bfloat16)
        index = lax.axis_index("head")
        for step in range(head_count):
            outs[step][...] = total[aligned(index ^ step, part), :]

    return pl.pallas_call(
        kernel,
        out_shape=[jax.ShapeDtypeStruct((part, chunks * width), jnp.bfloat16)] * head_count,
        scratch_shapes=[pltpu.VMEM((rows, chunks * width), jnp.bfloat16)],
        compiler_params=pltpu.CompilerParams(vmem_limit_bytes=32 << 20),
        cost_estimate=cost(4 * chunks * rows * width, 12 * chunks * rows * width),
        name="sum_kv",
    )(*[x for group in parts for x in group])


def join_grads(dq_parts, dkv_parts):
    chunks, head_count = len(dq_parts), len(dkv_parts)
    part, width = dq_parts[0][0].shape
    count = chunks * head_count

    def kernel(*refs):
        q_ins, kv_ins = refs[:count], refs[count : count + head_count]
        q_out, k_out, v_out = refs[count + head_count :]
        own = lax.axis_index("head")
        for chunk in range(chunks):
            for step in range(head_count):
                slot = (own ^ step) * chunks + chunk
                q_out[:, aligned(slot, width)] = q_ins[chunk * head_count + step][...]
                at = 2 * DH * chunk
                k_out[:, aligned(slot, DH)] = kv_ins[step][:, at : at + DH]
                v_out[:, aligned(slot, DH)] = kv_ins[step][:, at + DH : at + 2 * DH]

    kv_shape = jax.ShapeDtypeStruct((part, count * DH), jnp.bfloat16)
    return pl.pallas_call(
        kernel,
        out_shape=[jax.ShapeDtypeStruct((part, count * width), jnp.bfloat16), kv_shape, kv_shape],
        compiler_params=pltpu.CompilerParams(vmem_limit_bytes=32 << 20),
        cost_estimate=cost(0, 5 * part * count * width),
        name="join_grads",
    )(*[x for group in dq_parts for x in group], *dkv_parts)


def per_device(queries, keys, values, attn_out, out_grad, log_sum, file_ids):
    ctx_count = lax.axis_size("ctx")
    head_count = lax.axis_size("head")
    half = ctx_count // 2
    heads = log_sum.shape[0]
    chunks = keys.shape[1] // head_count // DH
    whole = (0, 1)

    def over_head(block, step):
        if step == 0:
            return block
        return lax.ppermute(block, "head", [(i, i ^ step) for i in range(head_count)])

    def over_ctx(block, step):
        pairs = [(i, i - i % half + (i % half ^ step)) for i in range(ctx_count)]
        return lax.ppermute(block, "ctx", pairs)

    steps = range(head_count)
    kv_packed = pack_kv(keys, values, head_count, chunks)
    queries, kv_packed = lax.optimization_barrier((queries, kv_packed))
    kv_parts = [over_head(kv_packed[step], step) for step in steps]
    packed = pack_q(queries, head_count, chunks, whole)
    packed, kv_parts = lax.optimization_barrier((packed, kv_parts))
    kv_joined = join_kv(kv_parts, file_ids, chunks)
    q_sent = {key: over_head(packed[key], key[0]) for key in packed}
    delta = row_deltas(out_grad, attn_out, heads)
    inputs = []
    for chunk in range(chunks):
        q_parts = [q_sent[step, 0 if step in whole else chunk] for step in steps]
        own = kv_joined[chunk]
        inputs.append((q_parts, [own] + [over_ctx(own, step) for step in range(1, half)]))

    dq_parts, dq_kept, dkv_parts = [], [], []
    for chunk in range(chunks):
        q_parts, kv_blocks = inputs[chunk]
        outs = chunk_grads(chunk, half, q_parts, out_grad, log_sum, delta, kv_blocks)
        if chunk + 1 < chunks:
            outs, inputs[chunk + 1] = lax.optimization_barrier((outs, inputs[chunk + 1]))
        if chunk:
            outs, dkv_parts, dq_parts = lax.optimization_barrier((outs, dkv_parts, dq_parts))
        back = [over_ctx(x, step) for step, x in enumerate(outs[head_count + 1 :], 1)]
        dkv_parts.append([outs[head_count]] + back)
        dq_sent = {step: over_head(outs[step], step) for step in steps if step not in whole}
        dq_kept.append([outs[step] for step in steps if step in whole])
        dq_parts.append(dq_sent)
    dq_parts = [
        [over_head(kept[step], step) if step in whole else sent[step] for step in steps]
        for kept, sent in zip(dq_kept, dq_parts)
    ]
    pieces = sum_kv(dkv_parts, head_count, half)
    return tuple(join_grads(dq_parts, [over_head(pieces[step], step) for step in steps]))


def solution(mesh):
    return jax.shard_map(
        per_device,
        mesh=mesh,
        in_specs=(
            P(("ctx", "head"), None),
            P(("ctx", "head"), None),
            P(("ctx", "head"), None),
            P("ctx", "head"),
            P("ctx", "head"),
            P("head", "ctx"),
            P("ctx"),
        ),
        out_specs=(P(("ctx", "head"), None), P(("ctx", "head"), None), P(("ctx", "head"), None)),
        check_vma=False,
    )
```

```python
import math

import jax
import jax.numpy as jnp
from jax import lax
from jax.experimental import pallas as pl
from jax.experimental.pallas import tpu as pltpu
from jax.sharding import PartitionSpec as P

DH = 128
TAG_ROWS = 16
SCORE_SCALE = 1.0 / math.sqrt(DH)
LOG2E = math.log2(math.e)
NT = (((1,), (1,)), ((), ()))
NN = (((1,), (0,)), ((), ()))
TN = (((0,), (0,)), ((), ()))


ANY = pl.BlockSpec(memory_space=pl.ANY)
VMEM = pl.BlockSpec(memory_space=pltpu.VMEM)


def dot(a, b, dims):
    return lax.dot_general(a, b, dims, preferred_element_type=jnp.float32)


def aligned(index, size):
    return pl.ds(pl.multiple_of(index * size, size), size)


def cost(flops, moved):
    return pl.CostEstimate(flops=flops, bytes_accessed=moved, transcendentals=0)


def row_deltas(out_grad, attn_out, heads):
    rows = out_grad.shape[0]

    def kernel(grad_ref, out_ref, delta_ref):
        for head in range(heads):
            cols = slice(head * DH, (head + 1) * DH)
            prod = grad_ref[:, cols].astype(jnp.float32) * out_ref[:, cols].astype(jnp.float32)
            delta_ref[head : head + 1, :] = jnp.sum(jnp.transpose(prod), axis=0, keepdims=True)

    return pl.pallas_call(
        kernel,
        out_shape=jax.ShapeDtypeStruct((heads, rows), jnp.float32),
        compiler_params=pltpu.CompilerParams(vmem_limit_bytes=32 << 20),
        cost_estimate=cost(4 * rows * heads * DH, 4 * rows * heads * DH),
        name="row_deltas",
    )(out_grad, attn_out)


def run_copies(pairs, sems):
    copies = [pltpu.make_async_copy(src, dst, sems.at[i]) for i, (src, dst) in enumerate(pairs)]
    for copy in copies:
        copy.start()
    for copy in copies:
        copy.wait()


def pack_heads(queries, keys, values, file_ids, head_count, chunks, whole):
    part, rows = queries.shape[0], file_ids.shape[1]
    width = queries.shape[1] // (head_count * chunks)
    layout = []
    for step in range(head_count):
        layout += [(step, 0, chunks)] if step in whole else [(step, c, 1) for c in range(chunks)]

    def kernel(q_ref, k_ref, v_ref, id_ref, *refs):
        kv_outs, q_outs = refs[:head_count], refs[head_count : head_count + len(layout)]
        tag_out, sems = refs[-2:]
        own = lax.axis_index("head")
        pairs = []
        for step in range(head_count):
            for chunk in range(chunks):
                cols = aligned((own ^ step) * chunks + chunk, DH)
                at = 2 * DH * chunk
                pairs.append((k_ref.at[:, cols], kv_outs[step].at[:, at : at + DH]))
                pairs.append((v_ref.at[:, cols], kv_outs[step].at[:, at + DH : at + 2 * DH]))
        for out, (step, chunk, count) in zip(q_outs, layout):
            first = pl.multiple_of(((own ^ step) * chunks + chunk) * width, width)
            pairs.append((q_ref.at[:, pl.ds(first, count * width)], out))
        line = lax.broadcasted_iota(jnp.int32, (TAG_ROWS, DH), 0)
        tags = id_ref[...].astype(jnp.float32)
        for column in range(0, 2 * DH, DH):
            value = jnp.zeros((TAG_ROWS, DH), jnp.float32)
            for first in range(column, rows, 2 * DH):
                value = jnp.where(line == first // (2 * DH), tags[:, first : first + DH], value)
            tag_out[:, column : column + DH] = value.astype(jnp.bfloat16)
        run_copies(pairs, sems)

    outs = pl.pallas_call(
        kernel,
        out_shape=[jax.ShapeDtypeStruct((part, 2 * chunks * DH), keys.dtype)] * head_count
        + [jax.ShapeDtypeStruct((part, count * width), queries.dtype) for _, _, count in layout]
        + [jax.ShapeDtypeStruct((TAG_ROWS, 2 * DH), jnp.bfloat16)],
        in_specs=[ANY] * 3 + [VMEM],
        scratch_shapes=[pltpu.SemaphoreType.DMA((2 * head_count * chunks + len(layout),))],
        cost_estimate=cost(0, 4 * (queries.size + 2 * keys.size)),
        name="pack_heads",
    )(queries, keys, values, file_ids)
    q_outs = outs[head_count:-1]
    return outs[:head_count], {(k[0], k[1]): out for out, k in zip(q_outs, layout)}, outs[-1]


def join_kv(parts, tags, chunks):
    head_count = len(parts)
    part, width = parts[0].shape[0], 2 * DH
    rows = part * head_count

    def kernel(tag_ref, *refs):
        ins, outs, sems = refs[:head_count], refs[head_count:-1], refs[-1]
        own = lax.axis_index("head")
        pairs = []
        for chunk, out in enumerate(outs):
            cols = slice(chunk * width, (chunk + 1) * width)
            for step in range(head_count):
                pairs.append((ins[step].at[:, cols], out.at[aligned(own ^ step, part)]))
            pairs.append((tag_ref, out.at[rows:]))
        run_copies(pairs, sems)

    shape = jax.ShapeDtypeStruct((rows + TAG_ROWS, width), parts[0].dtype)
    return pl.pallas_call(
        kernel,
        out_shape=[shape] * chunks,
        in_specs=[ANY] * (1 + head_count),
        scratch_shapes=[pltpu.SemaphoreType.DMA((chunks * (head_count + 1),))],
        cost_estimate=cost(0, 4 * rows * width * chunks),
        name="join_kv",
    )(tags, *parts)


def tile_grads(chunk, half, own_tile, q_parts, out_grad, log_sum, delta, kv_blocks, dq_in, final):
    head_count = len(q_parts)
    part, rows = q_parts[0].shape[0], out_grad.shape[0]
    width = min(x.shape[1] for x in q_parts)
    group = width // DH
    pair = 2 if group % 2 == 0 else 1
    slots = 1 if own_tile else half
    sum_in = [] if dq_in is None else [dq_in]
    dq_count = head_count if final else 1
    dkv_count = 1 if own_tile else half - 1

    def kernel(*refs):
        refs = list(refs)
        lse_ref, delta_ref, g_ref = refs[:3]
        q_in = refs[3 : 3 + head_count]
        kv_refs = refs[3 + head_count : 3 + head_count + slots]
        refs = refs[3 + head_count + slots :]
        start_ref = refs.pop(0) if sum_in else None
        dq_out, dkv_out = refs[:dq_count], refs[dq_count : dq_count + dkv_count]
        q_buf, kv_buf, dkv_buf, dq_acc, dq_low, dk_acc, dv_acc, bias = refs[dq_count + dkv_count :]
        head_index = lax.axis_index("head")
        own = lax.rem(lax.axis_index("ctx"), half)
        for step, ref in enumerate(q_in):
            first = 0 if ref.shape[1] == width else chunk * width
            q_buf[aligned(head_index ^ step, part), :] = ref[:, first : first + width]
        for slot, ref in enumerate(kv_refs):
            kv_buf[slot] = ref[...]
        if sum_in:
            dq_acc[...] = start_ref[...]
        elif not own_tile:
            dq_acc[...] = jnp.zeros_like(dq_acc)

        def load_tags(slot):
            lines = kv_buf[slot, rows:, :].astype(jnp.float32)
            pieces = [
                lines[first // (2 * DH) : first // (2 * DH) + 1, : min(rows - first, 2 * DH)]
                for first in range(0, rows, 2 * DH)
            ]
            return jnp.concatenate(pieces, axis=1)

        own_tags = load_tags(0)

        def set_bias(tags, block):
            key_tags = jnp.transpose(jnp.broadcast_to(tags, (8, rows)))[:, :1]
            key_pos = block * rows + lax.broadcasted_iota(jnp.int32, (rows, rows), 0)
            query_pos = own * rows + lax.broadcasted_iota(jnp.int32, (rows, rows), 1)
            allowed = (key_tags == own_tags) & (key_pos <= query_pos)
            bias[...] = jnp.where(allowed, 0.0, -1e30)

        def tile(slot, masked, strips):
            for first in range(0, group, pair):
                heads_here = [chunk * group + first + i for i in range(pair)]
                columns = [slice((first + i) * DH, (first + i + 1) * DH) for i in range(pair)]
                for top, bottom, left in strips:
                    count = rows - left
                    key = kv_buf[slot, top:bottom, :DH]
                    value = kv_buf[slot, top:bottom, DH:]

                    def side(pieces, axis):
                        return jnp.concatenate(pieces, axis=axis)

                    query = side([q_buf[left:, cols] for cols in columns], 0)
                    grad = side([g_ref[left:, h * DH : (h + 1) * DH] for h in heads_here], 0)
                    lse = side([lse_ref[h : h + 1, left:] for h in heads_here], 1) * LOG2E
                    shift = side([delta_ref[h : h + 1, left:] for h in heads_here], 1)
                    scores = dot(key, query, NT) * (SCORE_SCALE * LOG2E) - lse
                    if masked:
                        scores = scores + side([bias[top:bottom, left:]] * pair, 1)
                    probs = jnp.exp2(scores)
                    dprobs = dot(value, grad, NT)
                    dscores = (probs * (dprobs - shift)).astype(jnp.bfloat16)
                    dv_part = dot(probs.astype(jnp.bfloat16), grad, NN)
                    dk_part = dot(dscores, query, NN)
                    dq_part = dot(key, dscores, TN)
                    if first == 0:
                        dv_acc[top:bottom, :] = dv_part
                        dk_acc[top:bottom, :] = dk_part
                    else:
                        dv_acc[top:bottom, :] += dv_part
                        dk_acc[top:bottom, :] += dk_part
                    for i, cols in enumerate(columns):
                        piece = dq_part[:, i * count : (i + 1) * count]
                        if own_tile and not sum_in and left == 0:
                            dq_acc[cols, :] = piece
                        else:
                            dq_acc[cols, left:] += piece

        if own_tile:
            set_bias(own_tags, own)
            tile(0, True, [(top, top + DH, top) for top in range(0, rows, DH)])
            dkv_out[0][:, :DH] = dk_acc[...] * SCORE_SCALE
            dkv_out[0][:, DH:] = dv_acc[...]
        else:
            own_low, own_high = jnp.min(own_tags), jnp.max(own_tags)
            whole_tile = [(0, rows, 0)]

            def store(slot):
                dkv_buf[slot, :, :DH] = (dk_acc[...] * SCORE_SCALE).astype(jnp.bfloat16)
                dkv_buf[slot, :, DH:] = dv_acc[...].astype(jnp.bfloat16)

            def visit(slot, _):
                block = own ^ slot

                @pl.when(block < own)
                def _():
                    tags = load_tags(slot)
                    needed = jnp.max(tags) == own_low
                    full = jnp.min(tags) == own_high

                    @pl.when(full)
                    def _():
                        tile(slot, False, whole_tile)
                        store(slot)

                    @pl.when(jnp.logical_not(full) & needed)
                    def _():
                        set_bias(tags, block)
                        tile(slot, True, whole_tile)
                        store(slot)

                    @pl.when(jnp.logical_not(full | needed))
                    def _():
                        dkv_buf[slot] = jnp.zeros(dkv_buf.shape[1:], dkv_buf.dtype)

                return 0

            lax.fori_loop(1, slots, visit, 0)
            for slot in range(1, slots):
                @pl.when((own ^ slot) < own)
                def _():
                    dkv_out[slot - 1][...] = dkv_buf[slot]

        if final:
            for member in range(group):
                cols = slice(member * DH, (member + 1) * DH)
                low = (dq_acc[cols, :] * SCORE_SCALE).astype(dq_low.dtype)
                dq_low[:, cols] = jnp.transpose(low)
            for step in range(head_count):
                dq_out[step][...] = dq_low[aligned(head_index ^ step, part), :]
        else:
            dq_out[0][...] = dq_acc[...]

    bf16, f32 = jnp.bfloat16, jnp.float32
    dq_shape = jax.ShapeDtypeStruct((part, width), bf16)
    if not final:
        dq_shape = jax.ShapeDtypeStruct((width, rows), f32)
    dkv_shape = jax.ShapeDtypeStruct((rows, 2 * DH), f32 if own_tile else bf16)
    outs = pl.pallas_call(
        kernel,
        out_shape=[dq_shape] * dq_count + [dkv_shape] * dkv_count,
        scratch_shapes=[
            pltpu.VMEM((rows, width), bf16),
            pltpu.VMEM((slots,) + kv_blocks[0].shape, bf16),
            pltpu.VMEM((slots, rows, 2 * DH), bf16),
            pltpu.VMEM((width, rows), f32),
            pltpu.VMEM((rows, width), bf16),
            pltpu.VMEM((rows, DH), f32),
            pltpu.VMEM((rows, DH), f32),
            pltpu.VMEM((rows, rows), f32),
        ],
        compiler_params=pltpu.CompilerParams(vmem_limit_bytes=32 << 20),
        cost_estimate=pl.CostEstimate(
            flops=10 * rows * rows * width * dkv_count,
            bytes_accessed=8 * rows * width + 8 * slots * rows * 2 * DH,
            transcendentals=rows * rows * group * dkv_count,
        ),
        name="own_tile" if own_tile else "earlier_tiles",
    )(log_sum, delta, out_grad, *q_parts, *kv_blocks[:slots], *sum_in)
    return outs[:dq_count], outs[dq_count:]


def sum_kv(parts, head_count, half):
    chunks, count = len(parts), len(parts[0])
    rows, width = parts[0][0].shape
    part = rows // head_count

    def kernel(*refs):
        ins, outs, total = refs[: chunks * count], refs[chunks * count : -1], refs[-1]
        block = lax.rem(lax.axis_index("ctx"), half)
        for chunk in range(chunks):
            value = ins[chunk * count][...]
            for step in range(1, count):
                later = jnp.full((1, width), block ^ step, jnp.int32) > block
                sent = ins[chunk * count + step][...].astype(jnp.float32)
                value = value + jnp.where(later, sent, 0.0)
            total[:, chunk * width : (chunk + 1) * width] = value.astype(jnp.bfloat16)
        index = lax.axis_index("head")
        for step in range(head_count):
            outs[step][...] = total[aligned(index ^ step, part), :]

    return pl.pallas_call(
        kernel,
        out_shape=[jax.ShapeDtypeStruct((part, chunks * width), jnp.bfloat16)] * head_count,
        scratch_shapes=[pltpu.VMEM((rows, chunks * width), jnp.bfloat16)],
        compiler_params=pltpu.CompilerParams(vmem_limit_bytes=32 << 20),
        cost_estimate=cost(4 * chunks * rows * width, 12 * chunks * rows * width),
        name="sum_kv",
    )(*[x for group in parts for x in group])


def join_grads(dq_parts, dkv_parts):
    chunks, head_count = len(dq_parts), len(dkv_parts)
    part, width = dq_parts[0][0].shape
    count = chunks * head_count

    def kernel(*refs):
        q_ins, kv_ins = refs[:count], refs[count : count + head_count]
        q_out, k_out, v_out = refs[count + head_count :]
        own = lax.axis_index("head")
        for chunk in range(chunks):
            for step in range(head_count):
                slot = (own ^ step) * chunks + chunk
                q_out[:, aligned(slot, width)] = q_ins[chunk * head_count + step][...]
                at = 2 * DH * chunk
                k_out[:, aligned(slot, DH)] = kv_ins[step][:, at : at + DH]
                v_out[:, aligned(slot, DH)] = kv_ins[step][:, at + DH : at + 2 * DH]

    kv_shape = jax.ShapeDtypeStruct((part, count * DH), jnp.bfloat16)
    return pl.pallas_call(
        kernel,
        out_shape=[jax.ShapeDtypeStruct((part, count * width), jnp.bfloat16), kv_shape, kv_shape],
        compiler_params=pltpu.CompilerParams(vmem_limit_bytes=32 << 20),
        cost_estimate=cost(0, 5 * part * count * width),
        name="join_grads",
    )(*[x for group in dq_parts for x in group], *dkv_parts)


def per_device(queries, keys, values, attn_out, out_grad, log_sum, file_ids):
    ctx_count = lax.axis_size("ctx")
    head_count = lax.axis_size("head")
    half = ctx_count // 2
    heads = log_sum.shape[0]
    chunks = keys.shape[1] // head_count // DH
    whole = (0, 1)

    def over_head(block, step):
        if step == 0:
            return block
        return lax.ppermute(block, "head", [(i, i ^ step) for i in range(head_count)])

    def over_ctx(block, step):
        pairs = [(i, i - i % half + (i % half ^ step)) for i in range(ctx_count)]
        return lax.ppermute(block, "ctx", pairs)

    steps = range(head_count)
    kv_packed, packed, tags = pack_heads(
        queries, keys, values, file_ids[None, :], head_count, chunks, whole
    )
    kv_parts = [over_head(kv_packed[step], step) for step in steps]
    q_sent = {(step, 0): over_head(packed.pop((step, 0)), step) for step in whole}
    packed, kv_parts, tags, q_sent = lax.optimization_barrier((packed, kv_parts, tags, q_sent))
    kv_joined = join_kv(kv_parts, tags, chunks)
    q_sent.update({key: over_head(packed[key], key[0]) for key in packed})
    delta = row_deltas(out_grad, attn_out, heads)
    inputs = []
    for chunk in range(chunks):
        q_parts = [q_sent[step, 0 if step in whole else chunk] for step in steps]
        own = kv_joined[chunk]
        inputs.append((q_parts, [own] + [over_ctx(own, step) for step in range(1, half)]))

    dq_parts, dq_kept, dkv_parts = [], [], []
    for chunk in range(chunks):
        q_parts, kv_blocks = inputs[chunk]
        args = (q_parts, out_grad, log_sum, delta, kv_blocks)
        if chunk == 0:
            partial, (own_dkv,) = tile_grads(chunk, half, True, *args, None, False)
            dq, dkv = tile_grads(chunk, half, False, *args, partial[0], True)
            if chunks > 1:
                dq, dkv, inputs[1] = lax.optimization_barrier((dq, dkv, inputs[1]))
        else:
            partial, dkv = tile_grads(chunk, half, False, *args, None, False)
            partial, dkv, dkv_parts, dq_parts = lax.optimization_barrier(
                (partial, dkv, dkv_parts, dq_parts)
            )
            dq, (own_dkv,) = tile_grads(chunk, half, True, *args, partial[0], True)
            if chunk + 1 < chunks:
                dq, inputs[chunk + 1] = lax.optimization_barrier((dq, inputs[chunk + 1]))
        back = [over_ctx(x, step) for step, x in enumerate(dkv, 1)]
        dkv_parts.append([own_dkv] + back)
        dq_parts.append({step: over_head(dq[step], step) for step in steps if step not in whole})
        dq_kept.append([dq[step] for step in steps if step in whole])
    dq_kept, dkv_parts[-1] = lax.optimization_barrier((dq_kept, dkv_parts[-1]))
    dq_parts = [
        [over_head(kept[step], step) if step in whole else sent[step] for step in steps]
        for kept, sent in zip(dq_kept, dq_parts)
    ]
    pieces = sum_kv(dkv_parts, head_count, half)
    return tuple(join_grads(dq_parts, [over_head(pieces[step], step) for step in steps]))


def solution(mesh):
    return jax.shard_map(
        per_device,
        mesh=mesh,
        in_specs=(
            P(("ctx", "head"), None),
            P(("ctx", "head"), None),
            P(("ctx", "head"), None),
            P("ctx", "head"),
            P("ctx", "head"),
            P("head", "ctx"),
            P("ctx"),
        ),
        out_specs=(P(("ctx", "head"), None), P(("ctx", "head"), None), P(("ctx", "head"), None)),
        check_vma=False,
    )
```

```python
import math

import jax
import jax.numpy as jnp
from jax import lax
from jax.experimental import pallas as pl
from jax.experimental.pallas import tpu as pltpu
from jax.sharding import PartitionSpec as P

DH = 128
TAG_ROWS = 16
SCORE_SCALE = 1.0 / math.sqrt(DH)
LOG2E = math.log2(math.e)
NT = (((1,), (1,)), ((), ()))
NN = (((1,), (0,)), ((), ()))
TN = (((0,), (0,)), ((), ()))


ANY = pl.BlockSpec(memory_space=pl.ANY)
VMEM = pl.BlockSpec(memory_space=pltpu.VMEM)


def dot(a, b, dims):
    return lax.dot_general(a, b, dims, preferred_element_type=jnp.float32)


def aligned(index, size):
    return pl.ds(pl.multiple_of(index * size, size), size)


def cost(flops, moved):
    return pl.CostEstimate(flops=flops, bytes_accessed=moved, transcendentals=0)


def row_deltas(out_grad, attn_out, heads):
    rows = out_grad.shape[0]

    def kernel(grad_ref, out_ref, delta_ref):
        for head in range(heads):
            cols = slice(head * DH, (head + 1) * DH)
            prod = grad_ref[:, cols].astype(jnp.float32) * out_ref[:, cols].astype(jnp.float32)
            delta_ref[head : head + 1, :] = jnp.sum(jnp.transpose(prod), axis=0, keepdims=True)

    return pl.pallas_call(
        kernel,
        out_shape=jax.ShapeDtypeStruct((heads, rows), jnp.float32),
        compiler_params=pltpu.CompilerParams(vmem_limit_bytes=32 << 20),
        cost_estimate=cost(4 * rows * heads * DH, 4 * rows * heads * DH),
        name="row_deltas",
    )(out_grad, attn_out)


def run_copies(pairs, sems):
    copies = [pltpu.make_async_copy(src, dst, sems.at[i]) for i, (src, dst) in enumerate(pairs)]
    for copy in copies:
        copy.start()
    for copy in copies:
        copy.wait()


def pack_kv(keys, values, head_count, chunks):
    def kernel(k_ref, v_ref, *refs):
        outs, sems = refs[:-1], refs[-1]
        own = lax.axis_index("head")
        pairs = []
        for step in range(head_count):
            for chunk in range(chunks):
                cols = aligned((own ^ step) * chunks + chunk, DH)
                at = 2 * DH * chunk
                pairs.append((k_ref.at[:, cols], outs[step].at[:, at : at + DH]))
                pairs.append((v_ref.at[:, cols], outs[step].at[:, at + DH : at + 2 * DH]))
        run_copies(pairs, sems)

    return pl.pallas_call(
        kernel,
        out_shape=[jax.ShapeDtypeStruct((keys.shape[0], 2 * chunks * DH), keys.dtype)] * head_count,
        in_specs=[ANY] * 2,
        scratch_shapes=[pltpu.SemaphoreType.DMA((2 * head_count * chunks,))],
        cost_estimate=cost(0, 8 * keys.size),
        name="pack_kv",
    )(keys, values)


def pack_q(queries, head_count, chunks, whole):
    part, width = queries.shape[0], queries.shape[1] // (head_count * chunks)
    layout = []
    for step in range(head_count):
        layout += [(step, 0, chunks)] if step in whole else [(step, c, 1) for c in range(chunks)]

    def kernel(q_ref, *refs):
        outs, sems = refs[:-1], refs[-1]
        own = lax.axis_index("head")
        pairs = []
        for out, (step, chunk, count) in zip(outs, layout):
            first = pl.multiple_of(((own ^ step) * chunks + chunk) * width, width)
            pairs.append((q_ref.at[:, pl.ds(first, count * width)], out))
        run_copies(pairs, sems)

    outs = pl.pallas_call(
        kernel,
        out_shape=[
            jax.ShapeDtypeStruct((part, count * width), queries.dtype) for _, _, count in layout
        ],
        in_specs=[ANY],
        scratch_shapes=[pltpu.SemaphoreType.DMA((len(layout),))],
        cost_estimate=cost(0, 4 * queries.size),
        name="pack_q",
    )(queries)
    return {(step, chunk): out for out, (step, chunk, _) in zip(outs, layout)}


def join_kv(parts, tags, chunks):
    head_count = len(parts)
    part, width = parts[0].shape[0], 2 * DH
    rows = part * head_count

    def kernel(tag_ref, *refs):
        ins, outs, sems = refs[:head_count], refs[head_count:-1], refs[-1]
        own = lax.axis_index("head")
        pairs = []
        for chunk, out in enumerate(outs):
            cols = slice(chunk * width, (chunk + 1) * width)
            for step in range(head_count):
                pairs.append((ins[step].at[:, cols], out.at[aligned(own ^ step, part)]))
            pairs.append((tag_ref, out.at[rows:]))
        run_copies(pairs, sems)

    shape = jax.ShapeDtypeStruct((rows + TAG_ROWS, width), parts[0].dtype)
    return pl.pallas_call(
        kernel,
        out_shape=[shape] * chunks,
        in_specs=[ANY] * (1 + head_count),
        scratch_shapes=[pltpu.SemaphoreType.DMA((chunks * (head_count + 1),))],
        cost_estimate=cost(0, 4 * rows * width * chunks),
        name="join_kv",
    )(tags, *parts)


def tile_grads(chunk, half, own_tile, q_parts, out_grad, log_sum, delta, kv_blocks, dq_in, final):
    head_count = len(q_parts)
    part, rows = q_parts[0].shape[0], out_grad.shape[0]
    width = min(x.shape[1] for x in q_parts)
    group = width // DH
    pair = 2 if group % 2 == 0 else 1
    slots = 1 if own_tile else half
    sum_in = [] if dq_in is None else [dq_in]
    dq_count = head_count if final else 1
    dkv_count = 1 if own_tile else half - 1

    def kernel(*refs):
        refs = list(refs)
        lse_ref, delta_ref, g_ref = refs[:3]
        q_in = refs[3 : 3 + head_count]
        kv_refs = refs[3 + head_count : 3 + head_count + slots]
        refs = refs[3 + head_count + slots :]
        start_ref = refs.pop(0) if sum_in else None
        dq_out, dkv_out = refs[:dq_count], refs[dq_count : dq_count + dkv_count]
        q_buf, kv_buf, dkv_buf, dq_acc, dq_low, dk_acc, dv_acc, bias = refs[dq_count + dkv_count :]
        head_index = lax.axis_index("head")
        own = lax.rem(lax.axis_index("ctx"), half)
        for step, ref in enumerate(q_in):
            first = 0 if ref.shape[1] == width else chunk * width
            q_buf[aligned(head_index ^ step, part), :] = ref[:, first : first + width]
        for slot, ref in enumerate(kv_refs):
            kv_buf[slot] = ref[...]
        if sum_in:
            dq_acc[...] = start_ref[...]
        elif not own_tile:
            dq_acc[...] = jnp.zeros_like(dq_acc)

        def load_tags(slot):
            lines = kv_buf[slot, rows:, :].astype(jnp.float32)
            pieces = [
                lines[first // (2 * DH) : first // (2 * DH) + 1, : min(rows - first, 2 * DH)]
                for first in range(0, rows, 2 * DH)
            ]
            return jnp.concatenate(pieces, axis=1)

        own_tags = load_tags(0)

        def set_bias(tags, block):
            key_tags = jnp.transpose(jnp.broadcast_to(tags, (8, rows)))[:, :1]
            key_pos = block * rows + lax.broadcasted_iota(jnp.int32, (rows, rows), 0)
            query_pos = own * rows + lax.broadcasted_iota(jnp.int32, (rows, rows), 1)
            allowed = (key_tags == own_tags) & (key_pos <= query_pos)
            bias[...] = jnp.where(allowed, 0.0, -1e30)

        def tile(slot, masked, strips):
            for first in range(0, group, pair):
                heads_here = [chunk * group + first + i for i in range(pair)]
                columns = [slice((first + i) * DH, (first + i + 1) * DH) for i in range(pair)]
                for top, bottom, left in strips:
                    count = rows - left
                    key = kv_buf[slot, top:bottom, :DH]
                    value = kv_buf[slot, top:bottom, DH:]

                    def side(pieces, axis):
                        return jnp.concatenate(pieces, axis=axis)

                    query = side([q_buf[left:, cols] for cols in columns], 0)
                    grad = side([g_ref[left:, h * DH : (h + 1) * DH] for h in heads_here], 0)
                    lse = side([lse_ref[h : h + 1, left:] for h in heads_here], 1) * LOG2E
                    shift = side([delta_ref[h : h + 1, left:] for h in heads_here], 1)
                    scores = dot(key, query, NT) * (SCORE_SCALE * LOG2E) - lse
                    if masked:
                        scores = scores + side([bias[top:bottom, left:]] * pair, 1)
                    probs = jnp.exp2(scores)
                    dprobs = dot(value, grad, NT)
                    dscores = (probs * (dprobs - shift)).astype(jnp.bfloat16)
                    dv_part = dot(probs.astype(jnp.bfloat16), grad, NN)
                    dk_part = dot(dscores, query, NN)
                    dq_part = dot(key, dscores, TN)
                    if first == 0:
                        dv_acc[top:bottom, :] = dv_part
                        dk_acc[top:bottom, :] = dk_part
                    else:
                        dv_acc[top:bottom, :] += dv_part
                        dk_acc[top:bottom, :] += dk_part
                    for i, cols in enumerate(columns):
                        piece = dq_part[:, i * count : (i + 1) * count]
                        if own_tile and not sum_in and left == 0:
                            dq_acc[cols, :] = piece
                        else:
                            dq_acc[cols, left:] += piece

        if own_tile:
            set_bias(own_tags, own)
            tile(0, True, [(top, top + DH, top) for top in range(0, rows, DH)])
            dkv_out[0][:, :DH] = dk_acc[...] * SCORE_SCALE
            dkv_out[0][:, DH:] = dv_acc[...]
        else:
            own_low, own_high = jnp.min(own_tags), jnp.max(own_tags)
            whole_tile = [(0, rows, 0)]

            def store(slot):
                dkv_buf[slot, :, :DH] = (dk_acc[...] * SCORE_SCALE).astype(jnp.bfloat16)
                dkv_buf[slot, :, DH:] = dv_acc[...].astype(jnp.bfloat16)

            def visit(slot, _):
                block = own ^ slot

                @pl.when(block < own)
                def _():
                    tags = load_tags(slot)
                    needed = jnp.max(tags) == own_low
                    full = jnp.min(tags) == own_high

                    @pl.when(full)
                    def _():
                        tile(slot, False, whole_tile)
                        store(slot)

                    @pl.when(jnp.logical_not(full) & needed)
                    def _():
                        set_bias(tags, block)
                        tile(slot, True, whole_tile)
                        store(slot)

                    @pl.when(jnp.logical_not(full | needed))
                    def _():
                        dkv_buf[slot] = jnp.zeros(dkv_buf.shape[1:], dkv_buf.dtype)

                return 0

            lax.fori_loop(1, slots, visit, 0)
            for slot in range(1, slots):
                @pl.when((own ^ slot) < own)
                def _():
                    dkv_out[slot - 1][...] = dkv_buf[slot]

        if final:
            for member in range(group):
                cols = slice(member * DH, (member + 1) * DH)
                low = (dq_acc[cols, :] * SCORE_SCALE).astype(dq_low.dtype)
                dq_low[:, cols] = jnp.transpose(low)
            for step in range(head_count):
                dq_out[step][...] = dq_low[aligned(head_index ^ step, part), :]
        else:
            dq_out[0][...] = dq_acc[...]

    bf16, f32 = jnp.bfloat16, jnp.float32
    dq_shape = jax.ShapeDtypeStruct((part, width), bf16)
    if not final:
        dq_shape = jax.ShapeDtypeStruct((width, rows), f32)
    dkv_shape = jax.ShapeDtypeStruct((rows, 2 * DH), f32 if own_tile else bf16)
    outs = pl.pallas_call(
        kernel,
        out_shape=[dq_shape] * dq_count + [dkv_shape] * dkv_count,
        scratch_shapes=[
            pltpu.VMEM((rows, width), bf16),
            pltpu.VMEM((slots,) + kv_blocks[0].shape, bf16),
            pltpu.VMEM((slots, rows, 2 * DH), bf16),
            pltpu.VMEM((width, rows), f32),
            pltpu.VMEM((rows, width), bf16),
            pltpu.VMEM((rows, DH), f32),
            pltpu.VMEM((rows, DH), f32),
            pltpu.VMEM((rows, rows), f32),
        ],
        compiler_params=pltpu.CompilerParams(vmem_limit_bytes=32 << 20),
        cost_estimate=pl.CostEstimate(
            flops=10 * rows * rows * width * dkv_count,
            bytes_accessed=8 * rows * width + 8 * slots * rows * 2 * DH,
            transcendentals=rows * rows * group * dkv_count,
        ),
        name="own_tile" if own_tile else "earlier_tiles",
    )(log_sum, delta, out_grad, *q_parts, *kv_blocks[:slots], *sum_in)
    return outs[:dq_count], outs[dq_count:]


def sum_kv(parts, head_count, half):
    chunks, count = len(parts), len(parts[0])
    rows, width = parts[0][0].shape
    part = rows // head_count

    def kernel(*refs):
        ins, outs, total = refs[: chunks * count], refs[chunks * count : -1], refs[-1]
        block = lax.rem(lax.axis_index("ctx"), half)
        for chunk in range(chunks):
            value = ins[chunk * count][...]
            for step in range(1, count):
                later = jnp.full((1, width), block ^ step, jnp.int32) > block
                sent = ins[chunk * count + step][...].astype(jnp.float32)
                value = value + jnp.where(later, sent, 0.0)
            total[:, chunk * width : (chunk + 1) * width] = value.astype(jnp.bfloat16)
        index = lax.axis_index("head")
        for step in range(head_count):
            outs[step][...] = total[aligned(index ^ step, part), :]

    return pl.pallas_call(
        kernel,
        out_shape=[jax.ShapeDtypeStruct((part, chunks * width), jnp.bfloat16)] * head_count,
        scratch_shapes=[pltpu.VMEM((rows, chunks * width), jnp.bfloat16)],
        compiler_params=pltpu.CompilerParams(vmem_limit_bytes=32 << 20),
        cost_estimate=cost(4 * chunks * rows * width, 12 * chunks * rows * width),
        name="sum_kv",
    )(*[x for group in parts for x in group])


def join_grads(dq_parts, dkv_parts):
    chunks, head_count = len(dq_parts), len(dkv_parts)
    part, width = dq_parts[0][0].shape
    count = chunks * head_count

    def kernel(*refs):
        q_ins, kv_ins = refs[:count], refs[count : count + head_count]
        q_out, k_out, v_out = refs[count + head_count :]
        own = lax.axis_index("head")
        for chunk in range(chunks):
            for step in range(head_count):
                slot = (own ^ step) * chunks + chunk
                q_out[:, aligned(slot, width)] = q_ins[chunk * head_count + step][...]
                at = 2 * DH * chunk
                k_out[:, aligned(slot, DH)] = kv_ins[step][:, at : at + DH]
                v_out[:, aligned(slot, DH)] = kv_ins[step][:, at + DH : at + 2 * DH]

    kv_shape = jax.ShapeDtypeStruct((part, count * DH), jnp.bfloat16)
    return pl.pallas_call(
        kernel,
        out_shape=[jax.ShapeDtypeStruct((part, count * width), jnp.bfloat16), kv_shape, kv_shape],
        compiler_params=pltpu.CompilerParams(vmem_limit_bytes=32 << 20),
        cost_estimate=cost(0, 5 * part * count * width),
        name="join_grads",
    )(*[x for group in dq_parts for x in group], *dkv_parts)


def per_device(queries, keys, values, attn_out, out_grad, log_sum, file_ids):
    ctx_count = lax.axis_size("ctx")
    head_count = lax.axis_size("head")
    half = ctx_count // 2
    heads = log_sum.shape[0]
    chunks = keys.shape[1] // head_count // DH
    whole = (0, 1)

    def over_head(block, step):
        if step == 0:
            return block
        return lax.ppermute(block, "head", [(i, i ^ step) for i in range(head_count)])

    def over_ctx(block, step):
        pairs = [(i, i - i % half + (i % half ^ step)) for i in range(ctx_count)]
        return lax.ppermute(block, "ctx", pairs)

    steps = range(head_count)
    kv_packed = pack_kv(keys, values, head_count, chunks)
    queries, kv_packed, file_ids = lax.optimization_barrier((queries, kv_packed, file_ids))
    kv_parts = [over_head(kv_packed[step], step) for step in steps]
    packed = pack_q(queries, head_count, chunks, whole)
    rows = file_ids.shape[0]
    tags = jnp.pad(file_ids.astype(jnp.bfloat16), (0, TAG_ROWS * 2 * DH - rows))
    tags = tags.reshape(TAG_ROWS, 2 * DH)
    packed, kv_parts, tags = lax.optimization_barrier((packed, kv_parts, tags))
    kv_joined = join_kv(kv_parts, tags, chunks)
    q_sent = {key: over_head(packed[key], key[0]) for key in packed}
    near = {(step, 0): q_sent.pop((step, 0)) for step in whole}
    kv_joined, near = lax.optimization_barrier((kv_joined, near))
    q_sent.update(near)
    delta = row_deltas(out_grad, attn_out, heads)
    inputs = []
    for chunk in range(chunks):
        q_parts = [q_sent[step, 0 if step in whole else chunk] for step in steps]
        own = kv_joined[chunk]
        inputs.append((q_parts, [own] + [over_ctx(own, step) for step in range(1, half)]))

    dq_parts, dq_kept, dkv_parts = [], [], []
    for chunk in range(chunks):
        q_parts, kv_blocks = inputs[chunk]
        args = (q_parts, out_grad, log_sum, delta, kv_blocks)
        if chunk == 0:
            partial, (own_dkv,) = tile_grads(chunk, half, True, *args, None, False)
            dq, dkv = tile_grads(chunk, half, False, *args, partial[0], True)
            if chunks > 1:
                dq, dkv, inputs[1] = lax.optimization_barrier((dq, dkv, inputs[1]))
        else:
            partial, dkv = tile_grads(chunk, half, False, *args, None, False)
            partial, dkv, dkv_parts, dq_parts = lax.optimization_barrier(
                (partial, dkv, dkv_parts, dq_parts)
            )
            dq, (own_dkv,) = tile_grads(chunk, half, True, *args, partial[0], True)
            if chunk + 1 < chunks:
                dq, inputs[chunk + 1] = lax.optimization_barrier((dq, inputs[chunk + 1]))
        back = [over_ctx(x, step) for step, x in enumerate(dkv, 1)]
        dkv_parts.append([own_dkv] + back)
        dq_parts.append({step: over_head(dq[step], step) for step in steps if step not in whole})
        dq_kept.append([dq[step] for step in steps if step in whole])
    dq_kept, dkv_parts[-1] = lax.optimization_barrier((dq_kept, dkv_parts[-1]))
    dq_kept = [[over_head(x, step) for step, x in zip(whole, kept)] for kept in dq_kept]
    pieces = sum_kv(dkv_parts, head_count, half)
    dq_parts = [
        [kept[step] if step in whole else sent[step] for step in steps]
        for kept, sent in zip(dq_kept, dq_parts)
    ]
    return tuple(join_grads(dq_parts, [over_head(pieces[step], step) for step in steps]))


def solution(mesh):
    return jax.shard_map(
        per_device,
        mesh=mesh,
        in_specs=(
            P(("ctx", "head"), None),
            P(("ctx", "head"), None),
            P(("ctx", "head"), None),
            P("ctx", "head"),
            P("ctx", "head"),
            P("head", "ctx"),
            P("ctx"),
        ),
        out_specs=(P(("ctx", "head"), None), P(("ctx", "head"), None), P(("ctx", "head"), None)),
        check_vma=False,
    )
```

```python
import math

import jax
import jax.numpy as jnp
from jax import lax
from jax.experimental import pallas as pl
from jax.experimental.pallas import tpu as pltpu
from jax.sharding import PartitionSpec as P

DH = 128
TAG_ROWS = 16
SCORE_SCALE = 1.0 / math.sqrt(DH)
LOG2E = math.log2(math.e)
NT = (((1,), (1,)), ((), ()))
NN = (((1,), (0,)), ((), ()))
TN = (((0,), (0,)), ((), ()))


ANY = pl.BlockSpec(memory_space=pl.ANY)
VMEM = pl.BlockSpec(memory_space=pltpu.VMEM)


def dot(a, b, dims):
    return lax.dot_general(a, b, dims, preferred_element_type=jnp.float32)


def aligned(index, size):
    return pl.ds(pl.multiple_of(index * size, size), size)


def cost(flops, moved):
    return pl.CostEstimate(flops=flops, bytes_accessed=moved, transcendentals=0)


def row_deltas(out_grad, attn_out, heads):
    rows = out_grad.shape[0]

    def kernel(grad_ref, out_ref, delta_ref):
        for head in range(heads):
            cols = slice(head * DH, (head + 1) * DH)
            prod = grad_ref[:, cols].astype(jnp.float32) * out_ref[:, cols].astype(jnp.float32)
            delta_ref[head : head + 1, :] = jnp.sum(jnp.transpose(prod), axis=0, keepdims=True)

    return pl.pallas_call(
        kernel,
        out_shape=jax.ShapeDtypeStruct((heads, rows), jnp.float32),
        compiler_params=pltpu.CompilerParams(vmem_limit_bytes=32 << 20),
        cost_estimate=cost(4 * rows * heads * DH, 4 * rows * heads * DH),
        name="row_deltas",
    )(out_grad, attn_out)


def run_copies(pairs, sems):
    copies = [pltpu.make_async_copy(src, dst, sems.at[i]) for i, (src, dst) in enumerate(pairs)]
    for copy in copies:
        copy.start()
    for copy in copies:
        copy.wait()


def pack_kv(keys, values, head_count, chunks):
    def kernel(k_ref, v_ref, *refs):
        outs, sems = refs[:-1], refs[-1]
        own = lax.axis_index("head")
        pairs = []
        for step in range(head_count):
            for chunk in range(chunks):
                cols = aligned((own ^ step) * chunks + chunk, DH)
                at = 2 * DH * chunk
                pairs.append((k_ref.at[:, cols], outs[step].at[:, at : at + DH]))
                pairs.append((v_ref.at[:, cols], outs[step].at[:, at + DH : at + 2 * DH]))
        run_copies(pairs, sems)

    return pl.pallas_call(
        kernel,
        out_shape=[jax.ShapeDtypeStruct((keys.shape[0], 2 * chunks * DH), keys.dtype)] * head_count,
        in_specs=[ANY] * 2,
        scratch_shapes=[pltpu.SemaphoreType.DMA((2 * head_count * chunks,))],
        cost_estimate=cost(0, 8 * keys.size),
        name="pack_kv",
    )(keys, values)


def pack_q(queries, head_count, chunks, whole):
    part, width = queries.shape[0], queries.shape[1] // (head_count * chunks)
    layout = []
    for step in range(head_count):
        layout += [(step, 0, chunks)] if step in whole else [(step, c, 1) for c in range(chunks)]

    def kernel(q_ref, *refs):
        outs, sems = refs[:-1], refs[-1]
        own = lax.axis_index("head")
        pairs = []
        for out, (step, chunk, count) in zip(outs, layout):
            first = pl.multiple_of(((own ^ step) * chunks + chunk) * width, width)
            pairs.append((q_ref.at[:, pl.ds(first, count * width)], out))
        run_copies(pairs, sems)

    outs = pl.pallas_call(
        kernel,
        out_shape=[
            jax.ShapeDtypeStruct((part, count * width), queries.dtype) for _, _, count in layout
        ],
        in_specs=[ANY],
        scratch_shapes=[pltpu.SemaphoreType.DMA((len(layout),))],
        compiler_params=pltpu.CompilerParams(vmem_limit_bytes=16 << 20),
        cost_estimate=cost(0, 4 * queries.size),
        name="pack_q",
    )(queries)
    return {(step, chunk): out for out, (step, chunk, _) in zip(outs, layout)}


def join_kv(parts, tags, chunks):
    head_count = len(parts)
    part, width = parts[0].shape[0], 2 * DH
    rows = part * head_count

    def kernel(tag_ref, *refs):
        ins, outs = refs[:head_count], refs[head_count:]
        own = lax.axis_index("head")
        for chunk, out in enumerate(outs):
            for step in range(head_count):
                out[aligned(own ^ step, part), :] = ins[step][:, chunk * width : (chunk + 1) * width]
            out[rows:, :] = tag_ref[...]

    shape = jax.ShapeDtypeStruct((rows + TAG_ROWS, width), parts[0].dtype)
    return pl.pallas_call(
        kernel,
        out_shape=[shape] * chunks,
        compiler_params=pltpu.CompilerParams(vmem_limit_bytes=16 << 20),
        cost_estimate=cost(0, 4 * rows * width * chunks),
        name="join_kv",
    )(tags, *parts)


def tile_grads(chunk, half, own_tile, q_parts, out_grad, log_sum, delta, kv_blocks, dq_in, final):
    head_count = len(q_parts)
    part, rows = q_parts[0].shape[0], out_grad.shape[0]
    width = min(x.shape[1] for x in q_parts)
    group = width // DH
    pair = 2 if group % 2 == 0 else 1
    slots = 1 if own_tile else half
    sum_in = [] if dq_in is None else [dq_in]
    dq_count = head_count if final else 1
    dkv_count = 1 if own_tile else half - 1

    def kernel(*refs):
        refs = list(refs)
        lse_ref, delta_ref, g_ref = refs[:3]
        q_in = refs[3 : 3 + head_count]
        kv_refs = refs[3 + head_count : 3 + head_count + slots]
        refs = refs[3 + head_count + slots :]
        start_ref = refs.pop(0) if sum_in else None
        dq_out, dkv_out = refs[:dq_count], refs[dq_count : dq_count + dkv_count]
        q_buf, kv_buf, dkv_buf, dq_acc, dq_low, dk_acc, dv_acc, bias = refs[dq_count + dkv_count :]
        dq_acc = dq_acc if final else dq_out[0]
        head_index = lax.axis_index("head")
        own = lax.rem(lax.axis_index("ctx"), half)
        for step, ref in enumerate(q_in):
            first = 0 if ref.shape[1] == width else chunk * width
            q_buf[aligned(head_index ^ step, part), :] = ref[:, first : first + width]
        for slot, ref in enumerate(kv_refs):
            kv_buf[slot] = ref[...]
        if sum_in:
            dq_acc[...] = start_ref[...]
        elif not own_tile:
            dq_acc[...] = jnp.zeros_like(dq_acc)

        def load_tags(slot):
            lines = kv_buf[slot, rows:, :].astype(jnp.float32)
            pieces = [
                lines[first // (2 * DH) : first // (2 * DH) + 1, : min(rows - first, 2 * DH)]
                for first in range(0, rows, 2 * DH)
            ]
            return jnp.concatenate(pieces, axis=1)

        own_tags = load_tags(0)

        def set_bias(tags, block):
            key_tags = jnp.transpose(jnp.broadcast_to(tags, (8, rows)))[:, :1]
            key_pos = block * rows + lax.broadcasted_iota(jnp.int32, (rows, rows), 0)
            query_pos = own * rows + lax.broadcasted_iota(jnp.int32, (rows, rows), 1)
            allowed = (key_tags == own_tags) & (key_pos <= query_pos)
            bias[...] = jnp.where(allowed, 0.0, -1e30)

        def tile(slot, masked, strips):
            for first in range(0, group, pair):
                heads_here = [chunk * group + first + i for i in range(pair)]
                columns = [slice((first + i) * DH, (first + i + 1) * DH) for i in range(pair)]
                for top, bottom, left in strips:
                    count = rows - left
                    key = kv_buf[slot, top:bottom, :DH]
                    value = kv_buf[slot, top:bottom, DH:]

                    def side(pieces, axis):
                        return jnp.concatenate(pieces, axis=axis)

                    query = side([q_buf[left:, cols] for cols in columns], 0)
                    grad = side([g_ref[left:, h * DH : (h + 1) * DH] for h in heads_here], 0)
                    lse = side([lse_ref[h : h + 1, left:] for h in heads_here], 1) * LOG2E
                    shift = side([delta_ref[h : h + 1, left:] for h in heads_here], 1)
                    scores = dot(key, query, NT) * (SCORE_SCALE * LOG2E) - lse
                    if masked:
                        scores = scores + side([bias[top:bottom, left:]] * pair, 1)
                    probs = jnp.exp2(scores)
                    dprobs = dot(value, grad, NT)
                    dscores = (probs * (dprobs - shift)).astype(jnp.bfloat16)
                    dv_part = dot(probs.astype(jnp.bfloat16), grad, NN)
                    dk_part = dot(dscores, query, NN)
                    dq_part = dot(key, dscores, TN)
                    if first == 0:
                        dv_acc[top:bottom, :] = dv_part
                        dk_acc[top:bottom, :] = dk_part
                    else:
                        dv_acc[top:bottom, :] += dv_part
                        dk_acc[top:bottom, :] += dk_part
                    for i, cols in enumerate(columns):
                        piece = dq_part[:, i * count : (i + 1) * count]
                        if own_tile and not sum_in and left == 0:
                            dq_acc[cols, :] = piece
                        else:
                            dq_acc[cols, left:] += piece

        if own_tile:
            set_bias(own_tags, own)
            tile(0, True, [(top, top + DH, top) for top in range(0, rows, DH)])
            dkv_out[0][:, :DH] = dk_acc[...] * SCORE_SCALE
            dkv_out[0][:, DH:] = dv_acc[...]
        else:
            own_low, own_high = jnp.min(own_tags), jnp.max(own_tags)
            whole_tile = [(0, rows, 0)]

            def store(slot):
                dkv_buf[slot, :, :DH] = (dk_acc[...] * SCORE_SCALE).astype(jnp.bfloat16)
                dkv_buf[slot, :, DH:] = dv_acc[...].astype(jnp.bfloat16)

            def visit(slot, _):
                block = own ^ slot

                @pl.when(block < own)
                def _():
                    tags = load_tags(slot)
                    needed = jnp.max(tags) == own_low
                    full = jnp.min(tags) == own_high

                    @pl.when(full)
                    def _():
                        tile(slot, False, whole_tile)
                        store(slot)

                    @pl.when(jnp.logical_not(full) & needed)
                    def _():
                        set_bias(tags, block)
                        tile(slot, True, whole_tile)
                        store(slot)

                    @pl.when(jnp.logical_not(full | needed))
                    def _():
                        dkv_buf[slot] = jnp.zeros(dkv_buf.shape[1:], dkv_buf.dtype)

                return 0

            lax.fori_loop(1, slots, visit, 0)
            for slot in range(1, slots):
                @pl.when((own ^ slot) < own)
                def _():
                    dkv_out[slot - 1][...] = dkv_buf[slot]

        if final:
            for member in range(group):
                cols = slice(member * DH, (member + 1) * DH)
                low = (dq_acc[cols, :] * SCORE_SCALE).astype(dq_low.dtype)
                dq_low[:, cols] = jnp.transpose(low)
            for step in range(head_count):
                dq_out[step][...] = dq_low[aligned(head_index ^ step, part), :]

    bf16, f32 = jnp.bfloat16, jnp.float32
    dq_shape = jax.ShapeDtypeStruct((part, width), bf16)
    if not final:
        dq_shape = jax.ShapeDtypeStruct((width, rows), f32)
    dkv_shape = jax.ShapeDtypeStruct((rows, 2 * DH), f32 if own_tile else bf16)
    outs = pl.pallas_call(
        kernel,
        out_shape=[dq_shape] * dq_count + [dkv_shape] * dkv_count,
        scratch_shapes=[
            pltpu.VMEM((rows, width), bf16),
            pltpu.VMEM((slots,) + kv_blocks[0].shape, bf16),
            pltpu.VMEM((slots, rows, 2 * DH), bf16),
            pltpu.VMEM((width, rows), f32),
            pltpu.VMEM((rows, width), bf16),
            pltpu.VMEM((rows, DH), f32),
            pltpu.VMEM((rows, DH), f32),
            pltpu.VMEM((rows, rows), f32),
        ],
        compiler_params=pltpu.CompilerParams(vmem_limit_bytes=32 << 20),
        cost_estimate=pl.CostEstimate(
            flops=10 * rows * rows * width * dkv_count,
            bytes_accessed=8 * rows * width + 8 * slots * rows * 2 * DH,
            transcendentals=rows * rows * group * dkv_count,
        ),
        name="own_tile" if own_tile else "earlier_tiles",
    )(log_sum, delta, out_grad, *q_parts, *kv_blocks[:slots], *sum_in)
    return outs[:dq_count], outs[dq_count:]


def sum_kv(parts, head_count, half):
    chunks, count = len(parts), len(parts[0])
    rows, width = parts[0][0].shape
    part = rows // head_count

    def kernel(*refs):
        ins, outs, total = refs[: chunks * count], refs[chunks * count : -1], refs[-1]
        block = lax.rem(lax.axis_index("ctx"), half)
        for chunk in range(chunks):
            value = ins[chunk * count][...]
            for step in range(1, count):
                later = jnp.full((1, width), block ^ step, jnp.int32) > block
                sent = ins[chunk * count + step][...].astype(jnp.float32)
                value = value + jnp.where(later, sent, 0.0)
            total[:, chunk * width : (chunk + 1) * width] = value.astype(jnp.bfloat16)
        index = lax.axis_index("head")
        for step in range(head_count):
            outs[step][...] = total[aligned(index ^ step, part), :]

    return pl.pallas_call(
        kernel,
        out_shape=[jax.ShapeDtypeStruct((part, chunks * width), jnp.bfloat16)] * head_count,
        scratch_shapes=[pltpu.VMEM((rows, chunks * width), jnp.bfloat16)],
        compiler_params=pltpu.CompilerParams(vmem_limit_bytes=32 << 20),
        cost_estimate=cost(4 * chunks * rows * width, 12 * chunks * rows * width),
        name="sum_kv",
    )(*[x for group in parts for x in group])


def join_grads(dq_parts, dkv_parts):
    chunks, head_count = len(dq_parts), len(dkv_parts)
    part, width = dq_parts[0][0].shape
    count = chunks * head_count

    def kernel(*refs):
        q_ins, kv_ins = refs[:count], refs[count : count + head_count]
        q_out, k_out, v_out = refs[count + head_count :]
        own = lax.axis_index("head")
        for chunk in range(chunks):
            for step in range(head_count):
                slot = (own ^ step) * chunks + chunk
                q_out[:, aligned(slot, width)] = q_ins[chunk * head_count + step][...]
                at = 2 * DH * chunk
                k_out[:, aligned(slot, DH)] = kv_ins[step][:, at : at + DH]
                v_out[:, aligned(slot, DH)] = kv_ins[step][:, at + DH : at + 2 * DH]

    kv_shape = jax.ShapeDtypeStruct((part, count * DH), jnp.bfloat16)
    return pl.pallas_call(
        kernel,
        out_shape=[jax.ShapeDtypeStruct((part, count * width), jnp.bfloat16), kv_shape, kv_shape],
        compiler_params=pltpu.CompilerParams(vmem_limit_bytes=32 << 20),
        cost_estimate=cost(0, 5 * part * count * width),
        name="join_grads",
    )(*[x for group in dq_parts for x in group], *dkv_parts)


def per_device(queries, keys, values, attn_out, out_grad, log_sum, file_ids):
    ctx_count = lax.axis_size("ctx")
    head_count = lax.axis_size("head")
    half = ctx_count // 2
    heads = log_sum.shape[0]
    chunks = keys.shape[1] // head_count // DH
    whole = (0, 1)

    def over_head(block, step):
        if step == 0:
            return block
        return lax.ppermute(block, "head", [(i, i ^ step) for i in range(head_count)])

    def over_ctx(block, step):
        pairs = [(i, i - i % half + (i % half ^ step)) for i in range(ctx_count)]
        return lax.ppermute(block, "ctx", pairs)

    steps = range(head_count)
    kv_packed = pack_kv(keys, values, head_count, chunks)
    queries, kv_packed, file_ids = lax.optimization_barrier((queries, kv_packed, file_ids))
    kv_parts = [over_head(kv_packed[step], step) for step in steps]
    packed = pack_q(queries, head_count, chunks, whole)
    rows = file_ids.shape[0]
    tags = jnp.pad(file_ids.astype(jnp.bfloat16), (0, TAG_ROWS * 2 * DH - rows))
    tags = tags.reshape(TAG_ROWS, 2 * DH)
    packed, kv_parts, tags = lax.optimization_barrier((packed, kv_parts, tags))
    kv_joined = join_kv(kv_parts, tags, chunks)
    q_sent = {key: over_head(packed[key], key[0]) for key in packed}
    near = {(step, 0): q_sent.pop((step, 0)) for step in whole}
    kv_joined, near = lax.optimization_barrier((kv_joined, near))
    q_sent.update(near)
    delta = row_deltas(out_grad, attn_out, heads)
    inputs = []
    for chunk in range(chunks):
        q_parts = [q_sent[step, 0 if step in whole else chunk] for step in steps]
        own = kv_joined[chunk]
        inputs.append((q_parts, [own] + [over_ctx(own, step) for step in range(1, half)]))

    dq_parts, dq_kept, dkv_parts = [], [], []
    for chunk in range(chunks):
        q_parts, kv_blocks = inputs[chunk]
        args = (q_parts, out_grad, log_sum, delta, kv_blocks)
        if chunk == 0:
            partial, (own_dkv,) = tile_grads(chunk, half, True, *args, None, False)
            dq, dkv = tile_grads(chunk, half, False, *args, partial[0], True)
            if chunks > 1:
                dq, dkv, inputs[1] = lax.optimization_barrier((dq, dkv, inputs[1]))
        else:
            partial, dkv = tile_grads(chunk, half, False, *args, None, False)
            partial, dkv, dkv_parts, dq_parts = lax.optimization_barrier(
                (partial, dkv, dkv_parts, dq_parts)
            )
            dq, (own_dkv,) = tile_grads(chunk, half, True, *args, partial[0], True)
            if chunk + 1 < chunks:
                dq, inputs[chunk + 1] = lax.optimization_barrier((dq, inputs[chunk + 1]))
        back = [over_ctx(x, step) for step, x in enumerate(dkv, 1)]
        dkv_parts.append([own_dkv] + back)
        dq_parts.append({step: over_head(dq[step], step) for step in steps if step not in whole})
        dq_kept.append([dq[step] for step in steps if step in whole])
    dq_kept, dkv_parts[-1] = lax.optimization_barrier((dq_kept, dkv_parts[-1]))
    dq_kept = [[over_head(x, step) for step, x in zip(whole, kept)] for kept in dq_kept]
    pieces = sum_kv(dkv_parts, head_count, half)
    dq_parts = [
        [kept[step] if step in whole else sent[step] for step in steps]
        for kept, sent in zip(dq_kept, dq_parts)
    ]
    return tuple(join_grads(dq_parts, [over_head(pieces[step], step) for step in steps]))


def solution(mesh):
    return jax.shard_map(
        per_device,
        mesh=mesh,
        in_specs=(
            P(("ctx", "head"), None),
            P(("ctx", "head"), None),
            P(("ctx", "head"), None),
            P("ctx", "head"),
            P("ctx", "head"),
            P("head", "ctx"),
            P("ctx"),
        ),
        out_specs=(P(("ctx", "head"), None), P(("ctx", "head"), None), P(("ctx", "head"), None)),
        check_vma=False,
    )
```

```python
import math

import jax
import jax.numpy as jnp
from jax import lax
from jax.experimental import pallas as pl
from jax.experimental.pallas import tpu as pltpu
from jax.sharding import PartitionSpec as P

DH = 128
TAG_ROWS = 16
SCORE_SCALE = 1.0 / math.sqrt(DH)
LOG2E = math.log2(math.e)
NT = (((1,), (1,)), ((), ()))
NN = (((1,), (0,)), ((), ()))
TN = (((0,), (0,)), ((), ()))


ANY = pl.BlockSpec(memory_space=pl.ANY)
VMEM = pl.BlockSpec(memory_space=pltpu.VMEM)


def dot(a, b, dims):
    return lax.dot_general(a, b, dims, preferred_element_type=jnp.float32)


def aligned(index, size):
    return pl.ds(pl.multiple_of(index * size, size), size)


def cost(flops, moved):
    return pl.CostEstimate(flops=flops, bytes_accessed=moved, transcendentals=0)


def row_deltas(out_grad, attn_out, heads):
    rows = out_grad.shape[0]

    def kernel(grad_ref, out_ref, delta_ref):
        for head in range(heads):
            cols = slice(head * DH, (head + 1) * DH)
            prod = grad_ref[:, cols].astype(jnp.float32) * out_ref[:, cols].astype(jnp.float32)
            delta_ref[head : head + 1, :] = jnp.sum(jnp.transpose(prod), axis=0, keepdims=True)

    return pl.pallas_call(
        kernel,
        out_shape=jax.ShapeDtypeStruct((heads, rows), jnp.float32),
        compiler_params=pltpu.CompilerParams(vmem_limit_bytes=32 << 20),
        cost_estimate=cost(4 * rows * heads * DH, 4 * rows * heads * DH),
        name="row_deltas",
    )(out_grad, attn_out)


def run_copies(pairs, sems):
    copies = [pltpu.make_async_copy(src, dst, sems.at[i]) for i, (src, dst) in enumerate(pairs)]
    for copy in copies:
        copy.start()
    for copy in copies:
        copy.wait()


def pack_kv(keys, values, head_count, chunks):
    def kernel(k_ref, v_ref, *refs):
        outs, sems = refs[:-1], refs[-1]
        own = lax.axis_index("head")
        pairs = []
        for step in range(1, head_count):
            for chunk in range(chunks):
                cols = aligned((own ^ step) * chunks + chunk, DH)
                at = 2 * DH * chunk
                pairs.append((k_ref.at[:, cols], outs[step - 1].at[:, at : at + DH]))
                pairs.append((v_ref.at[:, cols], outs[step - 1].at[:, at + DH : at + 2 * DH]))
        run_copies(pairs, sems)

    return pl.pallas_call(
        kernel,
        out_shape=[jax.ShapeDtypeStruct((keys.shape[0], 2 * chunks * DH), keys.dtype)]
        * (head_count - 1),
        in_specs=[ANY] * 2,
        scratch_shapes=[pltpu.SemaphoreType.DMA((2 * (head_count - 1) * chunks,))],
        cost_estimate=cost(0, 8 * keys.size),
        name="pack_kv",
    )(keys, values)


def pack_q(queries, keys, values, head_count, chunks, whole):
    part, width = queries.shape[0], queries.shape[1] // (head_count * chunks)
    layout = []
    for step in range(head_count):
        layout += [(step, 0, chunks)] if step in whole else [(step, c, 1) for c in range(chunks)]

    def kernel(q_ref, k_ref, v_ref, *refs):
        outs, kv_out, sems = refs[:-2], refs[-2], refs[-1]
        own = lax.axis_index("head")
        pairs = []
        for out, (step, chunk, count) in zip(outs, layout):
            first = pl.multiple_of(((own ^ step) * chunks + chunk) * width, width)
            pairs.append((q_ref.at[:, pl.ds(first, count * width)], out))
        for chunk in range(chunks):
            cols = aligned(own * chunks + chunk, DH)
            at = 2 * DH * chunk
            pairs.append((k_ref.at[:, cols], kv_out.at[:, at : at + DH]))
            pairs.append((v_ref.at[:, cols], kv_out.at[:, at + DH : at + 2 * DH]))
        run_copies(pairs, sems)

    outs = pl.pallas_call(
        kernel,
        out_shape=[
            jax.ShapeDtypeStruct((part, count * width), queries.dtype) for _, _, count in layout
        ]
        + [jax.ShapeDtypeStruct((part, 2 * chunks * DH), keys.dtype)],
        in_specs=[ANY] * 3,
        scratch_shapes=[pltpu.SemaphoreType.DMA((len(layout) + 2 * chunks,))],
        compiler_params=pltpu.CompilerParams(vmem_limit_bytes=16 << 20),
        cost_estimate=cost(0, 4 * queries.size),
        name="pack_q",
    )(queries, keys, values)
    return {(step, chunk): out for out, (step, chunk, _) in zip(outs, layout)}, outs[-1]


def join_kv(parts, tags, chunks):
    head_count = len(parts)
    part, width = parts[0].shape[0], 2 * DH
    rows = part * head_count

    def kernel(tag_ref, *refs):
        ins, outs = refs[:head_count], refs[head_count:]
        own = lax.axis_index("head")
        for chunk, out in enumerate(outs):
            for step in range(head_count):
                out[aligned(own ^ step, part), :] = ins[step][:, chunk * width : (chunk + 1) * width]
            out[rows:, :] = tag_ref[...]

    shape = jax.ShapeDtypeStruct((rows + TAG_ROWS, width), parts[0].dtype)
    return pl.pallas_call(
        kernel,
        out_shape=[shape] * chunks,
        compiler_params=pltpu.CompilerParams(vmem_limit_bytes=16 << 20),
        cost_estimate=cost(0, 4 * rows * width * chunks),
        name="join_kv",
    )(tags, *parts)


def tile_grads(chunk, half, own_tile, q_parts, out_grad, log_sum, delta, kv_blocks, dq_in, final):
    head_count = len(q_parts)
    part, rows = q_parts[0].shape[0], out_grad.shape[0]
    width = min(x.shape[1] for x in q_parts)
    group = width // DH
    pair = 2 if group % 2 == 0 else 1
    slots = 1 if own_tile else half
    sum_in = [] if dq_in is None else [dq_in]
    dq_count = head_count if final else 1
    dkv_count = 1 if own_tile else half - 1

    def kernel(*refs):
        refs = list(refs)
        lse_ref, delta_ref, g_ref = refs[:3]
        q_in = refs[3 : 3 + head_count]
        kv_refs = refs[3 + head_count : 3 + head_count + slots]
        refs = refs[3 + head_count + slots :]
        start_ref = refs.pop(0) if sum_in else None
        dq_out, dkv_out = refs[:dq_count], refs[dq_count : dq_count + dkv_count]
        q_buf, kv_buf, dkv_buf, dq_acc, dq_low, dk_acc, dv_acc, bias = refs[dq_count + dkv_count :]
        dq_acc = dq_acc if final else dq_out[0]
        head_index = lax.axis_index("head")
        own = lax.rem(lax.axis_index("ctx"), half)
        for step, ref in enumerate(q_in):
            first = 0 if ref.shape[1] == width else chunk * width
            q_buf[aligned(head_index ^ step, part), :] = ref[:, first : first + width]
        for slot, ref in enumerate(kv_refs):
            kv_buf[slot] = ref[...]
        if sum_in:
            dq_acc[...] = start_ref[...]
        elif not own_tile:
            dq_acc[...] = jnp.zeros_like(dq_acc)

        def load_tags(slot):
            lines = kv_buf[slot, rows:, :].astype(jnp.float32)
            pieces = [
                lines[first // (2 * DH) : first // (2 * DH) + 1, : min(rows - first, 2 * DH)]
                for first in range(0, rows, 2 * DH)
            ]
            return jnp.concatenate(pieces, axis=1)

        own_tags = load_tags(0)

        def set_bias(tags, block):
            key_tags = jnp.transpose(jnp.broadcast_to(tags, (8, rows)))[:, :1]
            key_pos = block * rows + lax.broadcasted_iota(jnp.int32, (rows, rows), 0)
            query_pos = own * rows + lax.broadcasted_iota(jnp.int32, (rows, rows), 1)
            allowed = (key_tags == own_tags) & (key_pos <= query_pos)
            bias[...] = jnp.where(allowed, 0.0, -1e30)

        def tile(slot, masked, strips):
            for first in range(0, group, pair):
                heads_here = [chunk * group + first + i for i in range(pair)]
                columns = [slice((first + i) * DH, (first + i + 1) * DH) for i in range(pair)]
                for top, bottom, left in strips:
                    count = rows - left
                    key = kv_buf[slot, top:bottom, :DH]
                    value = kv_buf[slot, top:bottom, DH:]

                    def side(pieces, axis):
                        return jnp.concatenate(pieces, axis=axis)

                    query = side([q_buf[left:, cols] for cols in columns], 0)
                    grad = side([g_ref[left:, h * DH : (h + 1) * DH] for h in heads_here], 0)
                    lse = side([lse_ref[h : h + 1, left:] for h in heads_here], 1) * LOG2E
                    shift = side([delta_ref[h : h + 1, left:] for h in heads_here], 1)
                    scores = dot(key, query, NT) * (SCORE_SCALE * LOG2E) - lse
                    if masked:
                        scores = scores + side([bias[top:bottom, left:]] * pair, 1)
                    probs = jnp.exp2(scores)
                    dprobs = dot(value, grad, NT)
                    dscores = (probs * (dprobs - shift)).astype(jnp.bfloat16)
                    dv_part = dot(probs.astype(jnp.bfloat16), grad, NN)
                    dk_part = dot(dscores, query, NN)
                    dq_part = dot(key, dscores, TN)
                    if first == 0:
                        dv_acc[top:bottom, :] = dv_part
                        dk_acc[top:bottom, :] = dk_part
                    else:
                        dv_acc[top:bottom, :] += dv_part
                        dk_acc[top:bottom, :] += dk_part
                    for i, cols in enumerate(columns):
                        piece = dq_part[:, i * count : (i + 1) * count]
                        if own_tile and not sum_in and left == 0:
                            dq_acc[cols, :] = piece
                        else:
                            dq_acc[cols, left:] += piece

        if own_tile:
            set_bias(own_tags, own)
            tile(0, True, [(top, top + DH, top) for top in range(0, rows, DH)])
            dkv_out[0][:, :DH] = dk_acc[...] * SCORE_SCALE
            dkv_out[0][:, DH:] = dv_acc[...]
        else:
            own_low, own_high = jnp.min(own_tags), jnp.max(own_tags)
            whole_tile = [(0, rows, 0)]

            def store(slot):
                dkv_buf[slot, :, :DH] = (dk_acc[...] * SCORE_SCALE).astype(jnp.bfloat16)
                dkv_buf[slot, :, DH:] = dv_acc[...].astype(jnp.bfloat16)

            def visit(slot, _):
                block = own ^ slot

                @pl.when(block < own)
                def _():
                    tags = load_tags(slot)
                    needed = jnp.max(tags) == own_low
                    full = jnp.min(tags) == own_high

                    @pl.when(full)
                    def _():
                        tile(slot, False, whole_tile)
                        store(slot)

                    @pl.when(jnp.logical_not(full) & needed)
                    def _():
                        set_bias(tags, block)
                        tile(slot, True, whole_tile)
                        store(slot)

                    @pl.when(jnp.logical_not(full | needed))
                    def _():
                        dkv_buf[slot] = jnp.zeros(dkv_buf.shape[1:], dkv_buf.dtype)

                return 0

            lax.fori_loop(1, slots, visit, 0)
            for slot in range(1, slots):
                @pl.when((own ^ slot) < own)
                def _():
                    dkv_out[slot - 1][...] = dkv_buf[slot]

        if final:
            for member in range(group):
                cols = slice(member * DH, (member + 1) * DH)
                low = (dq_acc[cols, :] * SCORE_SCALE).astype(dq_low.dtype)
                dq_low[:, cols] = jnp.transpose(low)
            for step in range(head_count):
                dq_out[step][...] = dq_low[aligned(head_index ^ step, part), :]

    bf16, f32 = jnp.bfloat16, jnp.float32
    dq_shape = jax.ShapeDtypeStruct((part, width), bf16)
    if not final:
        dq_shape = jax.ShapeDtypeStruct((width, rows), f32)
    dkv_shape = jax.ShapeDtypeStruct((rows, 2 * DH), f32 if own_tile else bf16)
    outs = pl.pallas_call(
        kernel,
        out_shape=[dq_shape] * dq_count + [dkv_shape] * dkv_count,
        scratch_shapes=[
            pltpu.VMEM((rows, width), bf16),
            pltpu.VMEM((slots,) + kv_blocks[0].shape, bf16),
            pltpu.VMEM((slots, rows, 2 * DH), bf16),
            pltpu.VMEM((width, rows), f32),
            pltpu.VMEM((rows, width), bf16),
            pltpu.VMEM((rows, DH), f32),
            pltpu.VMEM((rows, DH), f32),
            pltpu.VMEM((rows, rows), f32),
        ],
        compiler_params=pltpu.CompilerParams(vmem_limit_bytes=32 << 20),
        cost_estimate=pl.CostEstimate(
            flops=10 * rows * rows * width * dkv_count,
            bytes_accessed=8 * rows * width + 8 * slots * rows * 2 * DH,
            transcendentals=rows * rows * group * dkv_count,
        ),
        name="own_tile" if own_tile else "earlier_tiles",
    )(log_sum, delta, out_grad, *q_parts, *kv_blocks[:slots], *sum_in)
    return outs[:dq_count], outs[dq_count:]


def sum_kv(parts, head_count, half):
    chunks, count = len(parts), len(parts[0])
    rows, width = parts[0][0].shape
    part = rows // head_count

    def kernel(*refs):
        ins, outs, total = refs[: chunks * count], refs[chunks * count : -1], refs[-1]
        block = lax.rem(lax.axis_index("ctx"), half)
        for chunk in range(chunks):
            value = ins[chunk * count][...]
            for step in range(1, count):
                later = jnp.full((1, width), block ^ step, jnp.int32) > block
                sent = ins[chunk * count + step][...].astype(jnp.float32)
                value = value + jnp.where(later, sent, 0.0)
            total[:, chunk * width : (chunk + 1) * width] = value.astype(jnp.bfloat16)
        index = lax.axis_index("head")
        for step in range(head_count):
            outs[step][...] = total[aligned(index ^ step, part), :]

    return pl.pallas_call(
        kernel,
        out_shape=[jax.ShapeDtypeStruct((part, chunks * width), jnp.bfloat16)] * head_count,
        scratch_shapes=[pltpu.VMEM((rows, chunks * width), jnp.bfloat16)],
        compiler_params=pltpu.CompilerParams(vmem_limit_bytes=32 << 20),
        cost_estimate=cost(4 * chunks * rows * width, 12 * chunks * rows * width),
        name="sum_kv",
    )(*[x for group in parts for x in group])


def join_grads(dq_parts, dkv_parts):
    chunks, head_count = len(dq_parts), len(dkv_parts)
    part, width = dq_parts[0][0].shape
    count = chunks * head_count

    def kernel(*refs):
        q_ins, kv_ins = refs[:count], refs[count : count + head_count]
        q_out, k_out, v_out = refs[count + head_count :]
        own = lax.axis_index("head")
        for chunk in range(chunks):
            for step in range(head_count):
                slot = (own ^ step) * chunks + chunk
                q_out[:, aligned(slot, width)] = q_ins[chunk * head_count + step][...]
                at = 2 * DH * chunk
                k_out[:, aligned(slot, DH)] = kv_ins[step][:, at : at + DH]
                v_out[:, aligned(slot, DH)] = kv_ins[step][:, at + DH : at + 2 * DH]

    kv_shape = jax.ShapeDtypeStruct((part, count * DH), jnp.bfloat16)
    return pl.pallas_call(
        kernel,
        out_shape=[jax.ShapeDtypeStruct((part, count * width), jnp.bfloat16), kv_shape, kv_shape],
        compiler_params=pltpu.CompilerParams(vmem_limit_bytes=32 << 20),
        cost_estimate=cost(0, 5 * part * count * width),
        name="join_grads",
    )(*[x for group in dq_parts for x in group], *dkv_parts)


def per_device(queries, keys, values, attn_out, out_grad, log_sum, file_ids):
    ctx_count = lax.axis_size("ctx")
    head_count = lax.axis_size("head")
    half = ctx_count // 2
    heads = log_sum.shape[0]
    chunks = keys.shape[1] // head_count // DH
    whole = (0, 1)

    def over_head(block, step):
        if step == 0:
            return block
        return lax.ppermute(block, "head", [(i, i ^ step) for i in range(head_count)])

    def over_ctx(block, step):
        pairs = [(i, i - i % half + (i % half ^ step)) for i in range(ctx_count)]
        return lax.ppermute(block, "ctx", pairs)

    steps = range(head_count)
    kv_packed = pack_kv(keys, values, head_count, chunks)
    queries, kv_packed, file_ids = lax.optimization_barrier((queries, kv_packed, file_ids))
    packed, kv_near = pack_q(queries, keys, values, head_count, chunks, whole)
    kv_parts = [kv_near] + [over_head(kv_packed[step - 1], step) for step in steps[1:]]
    rows = file_ids.shape[0]
    tags = jnp.pad(file_ids.astype(jnp.bfloat16), (0, TAG_ROWS * 2 * DH - rows))
    tags = tags.reshape(TAG_ROWS, 2 * DH)
    packed, kv_parts, tags = lax.optimization_barrier((packed, kv_parts, tags))
    kv_joined = join_kv(kv_parts, tags, chunks)
    q_sent = {key: over_head(packed[key], key[0]) for key in packed}
    near = {(step, 0): q_sent.pop((step, 0)) for step in whole}
    kv_joined, near = lax.optimization_barrier((kv_joined, near))
    q_sent.update(near)
    delta = row_deltas(out_grad, attn_out, heads)
    inputs = []
    for chunk in range(chunks):
        q_parts = [q_sent[step, 0 if step in whole else chunk] for step in steps]
        own = kv_joined[chunk]
        inputs.append((q_parts, [own] + [over_ctx(own, step) for step in range(1, half)]))

    dq_parts, dq_kept, dkv_parts = [], [], []
    for chunk in range(chunks):
        q_parts, kv_blocks = inputs[chunk]
        args = (q_parts, out_grad, log_sum, delta, kv_blocks)
        if chunk == 0:
            partial, (own_dkv,) = tile_grads(chunk, half, True, *args, None, False)
            dq, dkv = tile_grads(chunk, half, False, *args, partial[0], True)
            if chunks > 1:
                dq, dkv, inputs[1] = lax.optimization_barrier((dq, dkv, inputs[1]))
        else:
            partial, dkv = tile_grads(chunk, half, False, *args, None, False)
            partial, dkv, dkv_parts, dq_parts = lax.optimization_barrier(
                (partial, dkv, dkv_parts, dq_parts)
            )
            dq, (own_dkv,) = tile_grads(chunk, half, True, *args, partial[0], True)
            if chunk + 1 < chunks:
                dq, inputs[chunk + 1] = lax.optimization_barrier((dq, inputs[chunk + 1]))
        back = [over_ctx(x, step) for step, x in enumerate(dkv, 1)]
        dkv_parts.append([own_dkv] + back)
        dq_parts.append({step: over_head(dq[step], step) for step in steps if step not in whole})
        dq_kept.append([dq[step] for step in steps if step in whole])
    dq_kept, dkv_parts[-1] = lax.optimization_barrier((dq_kept, dkv_parts[-1]))
    dq_kept = [[over_head(x, step) for step, x in zip(whole, kept)] for kept in dq_kept]
    pieces = sum_kv(dkv_parts, head_count, half)
    dq_parts = [
        [kept[step] if step in whole else sent[step] for step in steps]
        for kept, sent in zip(dq_kept, dq_parts)
    ]
    return tuple(join_grads(dq_parts, [over_head(pieces[step], step) for step in steps]))


def solution(mesh):
    return jax.shard_map(
        per_device,
        mesh=mesh,
        in_specs=(
            P(("ctx", "head"), None),
            P(("ctx", "head"), None),
            P(("ctx", "head"), None),
            P("ctx", "head"),
            P("ctx", "head"),
            P("head", "ctx"),
            P("ctx"),
        ),
        out_specs=(P(("ctx", "head"), None), P(("ctx", "head"), None), P(("ctx", "head"), None)),
        check_vma=False,
    )
```
